512 devices in a mesh: tile: 128 (over z, y, core), filt: 2 (over x_hi), mc: 2 (over x_lo).
Axes of the slice: x: 4 (x_hi: 2, x_lo: 2; x = x_hi * 2 + x_lo), y: 8, z: 8, core: 2. Of those that a mesh axis runs over, the one named last changes fastest.
Arguments:
- sky_mean: float32 [128, 6, 256, 256], P('tile', 'filt'), may hold values from -6 to 6
- sky_log_scale: float32 [128, 6, 256, 256], P('tile', 'filt'), may hold values from -2.5 to -0.5
- noise_draw: bfloat16 [2, 128, 6, 256, 256], P('mc', 'tile', 'filt'), may hold values from -5 to 5
- observed: bfloat16 [128, 6, 256, 256], P('tile', 'filt'), may hold values from -6 to 6
- inv_var: bfloat16 [128, 6, 256, 256], P('tile', 'filt'), may hold values from 0.5 to 4
- intersections: int32 [128, 6, 3, 9], replicated, may hold values from -128 to 128, as said below
- counts: int32 [128, 6], replicated, may hold values from 1 to 3, as said below
- kernels: float32 [8, 2, 25], replicated, may hold values from 0 to 0.08
- psf_coeffs: bfloat16 [128, 6, 6, 3], replicated, may hold values from -0.5 to 1
- prior_prec: float32 [6, 6], replicated, as said below
Outputs:
- grad_mu: float32 [128, 6, 256, 256], P('tile', 'filt')
- grad_rho: float32 [128, 6, 256, 256], P('tile', 'filt')
The draws below stay inside these ranges and needn't reach their ends.
Inputs may be any that keep to these rules, and one draw needn't show every extreme that they name: `intersections`: for tile t and filter f the first counts[t, f] slots name distinct exposures within 2 of t; later slots hold values in the same ranges and are not used. Offsets lie in -128 .. 128 and kernel indices in 0 .. 7. counts[t, f] never exceeds the number of exposures within 2 of tile t. `prior_prec`: Symmetric; each diagonal entry exceeds the sum of the magnitudes of the other entries of its row.
All inputs are finite; a program needn't handle non-finite values.
Results may differ from the reference program's by a relative error of at most 0.00086.
Values may be sent and summed in bfloat16 or wider, within the bound.
A program may use at most 64 MiB of HBM per device.

```python
import math
import jax
import jax.numpy as jnp
from jax import lax

PIX = 256
FILTERS = 6
NB = 6
NBASIS = 8
HW = 12
K = 3
REACH = 2
TILES = 128
EXPOS = 128
MC = 2


def draw_intersections(key, part):
    window_len = 2 * REACH + 1
    tile_ids = jnp.arange(TILES, dtype=jnp.int32)[:, None, None]
    offsets = jnp.arange(window_len, dtype=jnp.int32)[None, None, :] - REACH
    target = tile_ids + offsets
    outside = (target < 0) | (target >= TILES)
    scores = jax.random.randint(jax.random.fold_in(key, 11), (TILES, FILTERS, window_len), 0, 1 << 20) * window_len
    scores = scores + jnp.arange(window_len, dtype=jnp.int32)[None, None, :]
    scores = scores + outside.astype(jnp.int32) * (1 << 26)
    ranked = jnp.argsort(scores, axis=2, stable=True)[:, :, :K].astype(jnp.int32)
    exposure = jnp.clip(tile_ids + ranked - REACH, 0, TILES - 1)
    shifts = jax.random.randint(jax.random.fold_in(key, 12), (TILES, FILTERS, K, 2), -(PIX // 2), PIX // 2 + 1)
    basis_ids = jax.random.randint(jax.random.fold_in(key, 13), (TILES, FILTERS, K, NB), 0, NBASIS)
    return jnp.concatenate([exposure[..., None], shifts, basis_ids], axis=3).astype(jnp.int32)


def draw_counts(key, part):
    tile_ids = jnp.arange(TILES, dtype=jnp.int32)[:, None]
    in_range = jnp.minimum(tile_ids, REACH) + jnp.minimum(TILES - 1 - tile_ids, REACH) + 1
    chosen = jax.random.randint(jax.random.fold_in(key, 21), (TILES, FILTERS), 1, K + 1)
    chosen = jnp.minimum(chosen, in_range)
    forced = (tile_ids == TILES // 2) & (jnp.arange(FILTERS, dtype=jnp.int32)[None, :] == 0)
    return jnp.where(forced, K, chosen).astype(jnp.int32)


def draw_prior_prec(key, part):
    raw_off = jax.random.uniform(jax.random.fold_in(key, 31), (FILTERS, FILTERS), jnp.float32, -0.25, 0.25)
    diag_values = jax.random.uniform(jax.random.fold_in(key, 32), (FILTERS,), jnp.float32, 1.5, 2.5)
    identity = jnp.eye(FILTERS, dtype=jnp.float32)
    symmetric = 0.5 * (raw_off + raw_off.T) * (1.0 - identity)
    return (symmetric + identity * diag_values[:, None]).astype(jnp.float32)


def steps_of(key, extent, pieces, smallest, largest):
    def one(axis_at, shards_of):
        steps = jax.random.uniform(jax.random.fold_in(jax.random.fold_in(key, 6), axis_at), (shards_of,), jnp.float32, smallest / len(pieces), largest / len(pieces))
        return jnp.repeat(jnp.exp(steps), extent[axis_at] // shards_of).reshape((-1,) + (1,) * (len(extent) - axis_at - 1))

    gain = one(*pieces[0])
    for cut in pieces[1:]:
        gain = gain * one(*cut)
    return gain


def bell_draw(own_key, dims, spread, most, split=(), kind=jnp.bfloat16):
    drawn = jax.random.normal(own_key, dims, jnp.float32) * spread
    if len(split) > 0:
        drawn = steps_of(own_key, dims, split, -0.22, 0.18) * drawn
    return jnp.clip(drawn, min=-most, max=most).astype(kind)


def setup_inputs(seed: int = 0) -> dict:
    seeds = jax.random.split(jax.random.key(seed), 11)
    return {
        "sky_mean": bell_draw(seeds[0], (TILES, FILTERS, PIX, PIX), 1.0, 6.0, ((0, 128), (1, 2)), jnp.float32),
        "sky_log_scale": jnp.clip(-2.5 + 2.0 * jax.random.uniform(seeds[1], (TILES, FILTERS, PIX, PIX), jnp.float32) ** steps_of(seeds[1], (TILES, FILTERS, PIX, PIX), ((0, 128), (1, 2)), -0.2, 0.2), -2.5, -0.5),
        "noise_draw": bell_draw(seeds[2], (MC, TILES, FILTERS, PIX, PIX), 1.0, 5.0, ((0, 2), (1, 128), (2, 2))),
        "observed": bell_draw(seeds[3], (EXPOS, FILTERS, PIX, PIX), 1.0, 6.0, ((0, 128), (1, 2))),
        "inv_var": jnp.clip(jnp.exp(math.log(4.0) - 2.0794415 * jax.random.uniform(seeds[4], (EXPOS, FILTERS, PIX, PIX), jnp.float32) ** steps_of(seeds[4], (EXPOS, FILTERS, PIX, PIX), ((0, 128), (1, 2)), -0.2, 0.2)), 0.5, 4.0).astype(jnp.bfloat16),
        "intersections": draw_intersections(jax.random.fold_in(seeds[10], 71), 0),
        "counts": draw_counts(jax.random.fold_in(seeds[10], 71), 0),
        "kernels": jnp.clip(jax.random.uniform(seeds[7], (NBASIS, 2, 2 * HW + 1), jnp.float32, 0.0, 0.08), 0.0, 0.08),
        "psf_coeffs": jnp.clip(jax.random.uniform(seeds[8], (EXPOS, FILTERS, NB, 3), jnp.float32, -0.5, 1.0), -0.5, 1.0).astype(jnp.bfloat16),
        "prior_prec": draw_prior_prec(jax.random.fold_in(seeds[10], 71), 0),
    }


def build_padded(kernels, tile_side):
    tap_count = kernels.shape[2]
    half_span = (tap_count - 1) // 2
    offsets = jnp.arange(tile_side)[:, None] - jnp.arange(tile_side)[None, :] + half_span
    summed = jnp.zeros((kernels.shape[0], 2, tile_side, tile_side), jnp.float32)
    for tap_id in range(tap_count):
        summed = summed + kernels[:, :, tap_id][:, :, None, None] * (offsets == tap_id).astype(jnp.float32)
    return jnp.pad(summed.astype(jnp.bfloat16), ((0, 0), (0, 0), (tile_side, tile_side), (0, 0)))


def shifted_basis(basis_pad, basis_id, side_id, offset, tile_side):
    starts = (basis_id.astype(jnp.int32), jnp.int32(side_id), (tile_side - offset).astype(jnp.int32), jnp.int32(0))
    return lax.dynamic_slice(basis_pad, starts, (1, 1, tile_side, tile_side))[0, 0]


def weight_map(coeff_row, tile_side):
    centred = (2.0 * jnp.arange(tile_side, dtype=jnp.float32) + 1.0 - tile_side) / tile_side
    coeff_f = coeff_row.astype(jnp.float32)
    return coeff_f[0] + coeff_f[1] * centred[:, None] + coeff_f[2] * centred[None, :]


def contribution(basis_pad, image, slot_entry, coeff_rows, tile_side):
    summed = jnp.zeros((tile_side, tile_side), jnp.float32)
    for component in range(NB):
        basis_id = slot_entry[3 + component]
        rows_matrix = shifted_basis(basis_pad, basis_id, 0, slot_entry[1], tile_side)
        cols_matrix = shifted_basis(basis_pad, basis_id, 1, slot_entry[2], tile_side)
        half_blur = jnp.dot(rows_matrix, image, preferred_element_type=jnp.float32).astype(jnp.bfloat16)
        blurred = lax.dot_general(half_blur, cols_matrix, (((1,), (1,)), ((), ())), preferred_element_type=jnp.float32)
        summed = summed + weight_map(coeff_rows[component], tile_side) * blurred
    return summed.astype(jnp.bfloat16)


def adjoint_term(basis_pad, resid_img, slot_entry, coeff_rows, tile_side):
    summed = jnp.zeros((tile_side, tile_side), jnp.float32)
    for component in range(NB):
        basis_id = slot_entry[3 + component]
        rows_matrix = shifted_basis(basis_pad, basis_id, 0, slot_entry[1], tile_side)
        cols_matrix = shifted_basis(basis_pad, basis_id, 1, slot_entry[2], tile_side)
        weighted = (weight_map(coeff_rows[component], tile_side) * resid_img.astype(jnp.float32)).astype(jnp.bfloat16)
        back_half = lax.dot_general(rows_matrix, weighted, (((0,), (0,)), ((), ())), preferred_element_type=jnp.float32).astype(jnp.bfloat16)
        summed = summed + jnp.dot(back_half, cols_matrix, preferred_element_type=jnp.float32)
    return summed


def reference(sky_mean, sky_log_scale, noise_draw, observed, inv_var, intersections, counts, kernels, psf_coeffs, prior_prec):
    tile_side = sky_mean.shape[2]
    n_tiles = sky_mean.shape[0]
    n_filters = sky_mean.shape[1]
    n_samples = noise_draw.shape[0]
    basis_pad = build_padded(kernels, tile_side)
    scale_map = jnp.exp(sky_log_scale)
    live = (jnp.arange(K, dtype=jnp.int32)[None, None, :] < counts[:, :, None]).astype(jnp.float32)
    filt_col = jnp.arange(n_filters, dtype=jnp.int32)[:, None]
    forward_slots = jax.vmap(contribution, (None, None, 0, 0, None))
    forward_all = jax.vmap(forward_slots, (None, 0, 0, 0, None))
    backward_slots = jax.vmap(adjoint_term, (None, 0, 0, 0, None))
    backward_all = jax.vmap(backward_slots, (None, 0, 0, 0, None))
    tile_ids = jnp.arange(n_tiles, dtype=jnp.int32)
    sum_mean = jnp.zeros(sky_mean.shape, jnp.float32)
    sum_scale = jnp.zeros(sky_mean.shape, jnp.float32)
    for sample_id in range(n_samples):
        eps_float = noise_draw[sample_id].astype(jnp.float32)
        sample = sky_mean + scale_map * eps_float
        sample_b = sample.astype(jnp.bfloat16)

        def forward_tile(predicted, tile_id):
            slot_rows = intersections[tile_id]
            coeffs = psf_coeffs[slot_rows[:, :, 0], filt_col]
            contrib = forward_all(basis_pad, sample_b[tile_id], slot_rows, coeffs, tile_side)
            masked = contrib.astype(jnp.float32) * live[tile_id][:, :, None, None]
            return predicted.at[slot_rows[:, :, 0], filt_col].add(masked), None

        predicted = lax.scan(forward_tile, jnp.zeros(sky_mean.shape, jnp.float32), tile_ids)[0]
        residual = (inv_var.astype(jnp.float32) * (observed.astype(jnp.float32) - predicted)).astype(jnp.bfloat16)

        def adjoint_tile(tile_id):
            slot_rows = intersections[tile_id]
            coeffs = psf_coeffs[slot_rows[:, :, 0], filt_col]
            resid_imgs = residual[slot_rows[:, :, 0], filt_col]
            terms = backward_all(basis_pad, resid_imgs, slot_rows, coeffs, tile_side)
            return jnp.sum(terms * live[tile_id][:, :, None, None], axis=1)

        data_grad = lax.map(adjoint_tile, tile_ids)
        prior_grad = jnp.einsum("fg,tgij->tfij", prior_prec, sample, precision=lax.Precision.HIGHEST)
        sample_grad = data_grad - prior_grad
        sum_mean = sum_mean + sample_grad
        sum_scale = sum_scale + sample_grad * scale_map * eps_float
    return sum_mean / n_samples, sum_scale / n_samples + 1.0
```

```python
import functools

import jax
import jax.numpy as jnp
from jax import lax
from jax.experimental import pallas as pl
from jax.experimental.pallas import tpu as pltpu
from jax.sharding import PartitionSpec as P

NB = 6
K = 3
REACH = 2
WINDOW = 2 * REACH + 1
MESH = pl.DeviceIdType.MESH
F32 = jnp.float32
BF16 = jnp.bfloat16


def dot(a, b):
    return jnp.dot(a, b, preferred_element_type=F32)


def band_rows(pat, a, side):
    half = side // 2
    start = (16 * a - 12) % half
    rolled = pltpu.roll(pat, start, 1) if start else pat
    lane = lax.broadcasted_iota(jnp.int32, rolled.shape, 1)
    zero = jnp.zeros_like(rolled)
    low = jnp.where(lane < half // 2, rolled, zero)
    high = jnp.where(lane >= half // 2, rolled, zero)
    blocks = half // 16
    if a == 0:
        return low, zero
    if a < blocks - 1:
        return rolled, zero
    if a <= blocks:
        return high, low
    if a < 2 * blocks - 1:
        return zero, rolled
    return zero, high


def kernel(
    tiles,
    taps_ref,
    itab,
    ftab,
    mean_hbm,
    lsc_hbm,
    noise_hbm,
    obs_hbm,
    ivar_hbm,
    mu_hbm,
    rho_hbm,
    mean,
    scale,
    noise,
    obs,
    ivar,
    diff,
    lrow,
    rmat,
    rmat_t,
    cmat,
    cmat_t,
    x_ref,
    blur,
    mixed,
    placed,
    own,
    send_p,
    recv_p,
    send_d,
    recv_d,
    send_q,
    recv_q,
    near0,
    near1,
    near2,
    moved,
    half,
    send_g,
    recv_g,
    e_ref,
    pri_mu,
    pri_rho,
    mu,
    rho,
    in_sem,
    out_sem,
    noise_sem,
    p_sem,
    d_sem,
    q_sem,
    rp_sem,
    ru_sem,
    rd_sem,
    relay_sem,
    g_sem,
    e_sem,
):
    filters, side = mean.shape[0], mean.shape[1]
    nbasis = rmat.shape[0]
    near = (near0, near1, near2)
    t = lax.axis_index("tile")
    s = lax.axis_index("mc")
    h = lax.axis_index("filt")
    sigma = 1 - 2 * lax.rem(t, 2)
    partner = {"tile": t + sigma}
    ahead = {"tile": lax.rem(t + 2 * sigma + tiles, tiles)}
    behind = {"tile": lax.rem(t - 2 * sigma + tiles, tiles)}
    twin = {"mc": 1 - s}
    across = {"filt": 1 - h, "mc": 1 - s}

    i_k, i_oy, i_ox, i_e, i_sel = 0, 54, 63, 72, 81
    f_c, f_a, f_p = 0, 162, 378

    def remote(src, dst, sem, f, to):
        return pltpu.make_async_remote_copy(
            src_ref=src,
            dst_ref=dst,
            send_sem=sem.at[0, f],
            recv_sem=sem.at[1, f],
            device_id=to,
            device_id_type=MESH,
        )

    loads = []
    for f in range(filters):
        loads.append(
            [
                pltpu.make_async_copy(noise_hbm.at[f], noise.at[s, f], in_sem.at[0, f]),
                pltpu.make_async_copy(mean_hbm.at[f], mean.at[f], in_sem.at[1, f]),
                pltpu.make_async_copy(lsc_hbm.at[f], scale.at[f], in_sem.at[2, f]),
            ]
        )
    late = [
        pltpu.make_async_copy(obs_hbm, obs, in_sem.at[3, 0]),
        pltpu.make_async_copy(ivar_hbm, ivar, in_sem.at[3, 1]),
    ]
    for group in loads:
        for copy in group:
            copy.start()
    for copy in late:
        copy.start()

    barrier = pltpu.get_barrier_semaphore()
    for to in (partner, ahead, behind, twin, across):
        pl.semaphore_signal(barrier, inc=1, device_id=to, device_id_type=MESH)

    rows_i = lax.broadcasted_iota(jnp.int32, (side, side), 0)
    cols_i = lax.broadcasted_iota(jnp.int32, (side, side), 1)
    diff[...] = rows_i - cols_i
    centre_i = lax.broadcasted_iota(jnp.int32, (side, 128), 0)
    lrow[...] = (2 * centre_i + 1 - side).astype(F32) * (1.0 / side)
    centre_j = lax.broadcasted_iota(jnp.int32, (1, side), 1)
    lcol = (2 * centre_j + 1 - side).astype(F32) * (1.0 / side)
    placed[K] = jnp.zeros((side, side), BF16)

    def build(dst, first, stride):
        def one(k, carry):
            row = taps_ref[pl.ds(first + stride * k, 1), :]
            pat = jnp.broadcast_to(row, (16, 128))
            pat = pltpu.roll(pat, 0, 1, stride=1, stride_axis=0)
            for a in range(side // 16):
                left, right = band_rows(pat, a, side)
                dst[k, 16 * a : 16 * a + 16, 0:128] = left.astype(BF16)
                dst[k, 16 * a : 16 * a + 16, 128:256] = right.astype(BF16)
            return carry

        lax.fori_loop(0, nbasis, one, 0)

    def build_flat(dst, first, stride):
        def one(k, carry):
            row = taps_ref[pl.ds(first + stride * k, 1), :]
            pat = jnp.broadcast_to(row, (16, 128))
            pat = pltpu.roll(pat, 0, 1, stride=1, stride_axis=0)
            for a in range(side // 16):
                left, right = band_rows(pat, a, side)
                at = pl.ds(pl.multiple_of(k * side + 16 * a, 16), 16)
                dst[at, 0:128] = left.astype(BF16)
                dst[at, 128:256] = right.astype(BF16)
            return carry

        lax.fori_loop(0, nbasis, one, 0)

    build(rmat, 2 * nbasis, 2)
    build(cmat_t, 1, 2)

    for f in range(filters):
        loads[f][0].wait()
    pl.semaphore_wait(barrier, 5)
    noise_out = remote(noise.at[s], noise.at[s], noise_sem, 0, twin)
    noise_out.start()

    chunk = 32
    chunks = side // chunk

    def over_rows(body):
        def one(r, carry):
            body(pl.ds(pl.multiple_of(r * chunk, chunk), chunk))
            return carry

        lax.fori_loop(0, chunks, one, 0)

    def shift_matrix(offset):
        return jnp.where(diff[...] == offset, 1.0, 0.0).astype(BF16)

    def forward(f):
        def sample_rows(rows):
            sc = jnp.exp(scale[f, rows, :])
            scale[f, rows, :] = sc
            x_ref[rows, :] = (mean[f, rows, :] + sc * noise[s, f, rows, :].astype(F32)).astype(BF16)

        over_rows(sample_rows)

        def blur_one(k, carry):
            hb = dot(rmat[k], x_ref[...]).astype(BF16)
            blur[k] = dot(hb, cmat_t[k])
            return carry

        lax.fori_loop(0, nbasis, blur_one, 0, unroll=2)

        def slot(q, carry):
            fq = f * K + q
            base = f_c + fq * NB * 3
            c0 = [ftab[base + 3 * b] for b in range(NB)]
            c1 = [ftab[base + 3 * b + 1] for b in range(NB)]
            c2 = [ftab[base + 3 * b + 2] for b in range(NB)]
            kb = [itab[i_k + fq * NB + b] for b in range(NB)]
            beta = [c2[b] * lcol for b in range(NB)]

            def mix_rows(rows):
                li = lrow[rows, :]
                alpha = [c0[b] + c1[b] * li for b in range(NB)]
                for lo in (0, 128):
                    acc = None
                    for b in range(NB):
                        term = (alpha[b] + beta[b][:, lo : lo + 128]) * blur[kb[b], rows, lo : lo + 128]
                        acc = term if acc is None else acc + term
                    mixed[rows, lo : lo + 128] = acc.astype(BF16)

            over_rows(mix_rows)
            oy = itab[i_oy + fq]
            ox = itab[i_ox + fq]
            part = dot(shift_matrix(oy), mixed[...]).astype(BF16)
            placed[q] = dot(part, shift_matrix(-ox)).astype(BF16)
            return carry

        lax.fori_loop(0, K, slot, 0)

        def pick(d):
            return placed[itab[i_sel + f * WINDOW + d]]

        own[f] = pick(REACH)
        send_p[f, 0] = pick(REACH + sigma)
        send_p[f, 1] = pick(REACH - sigma)
        send_d[f] = pick(REACH - 2 * sigma)
        send_q[f] = pick(REACH + 2 * sigma)

    def p_copy(f):
        return remote(send_p.at[f], recv_p.at[f], p_sem, f, partner)

    def d_copy(f):
        return remote(send_d.at[f], recv_d.at[f], d_sem, f, behind)

    def q_copy(f):
        return remote(send_q.at[f], recv_q.at[f], q_sem, f, ahead)

    def merge(f):
        p_copy(f).wait_recv()

        def rows_of(rows):
            joined = send_q[f, rows, :].astype(F32) + recv_p[f, 1, rows, :].astype(F32)
            send_q[f, rows, :] = joined.astype(BF16)

        over_rows(rows_of)
        q_copy(f).start()

    for f in range(filters):
        loads[f][1].wait()
        loads[f][2].wait()
        forward(f)
        p_copy(f).start()
        d_copy(f).start()
        if f > 0:
            merge(f - 1)
    merge(filters - 1)

    noise_out.wait_recv()

    def g_copy(f):
        return remote(send_g.at[f], recv_g.at[f], g_sem, f, across)

    for f in range(filters):

        def twin_rows(rows):
            other = noise[1 - s, f, rows, :].astype(F32)
            send_g[f, rows, :] = (mean[f, rows, :] + scale[f, rows, :] * other).astype(BF16)

        over_rows(twin_rows)
        g_copy(f).start()

    build(rmat_t, 0, 2)
    build_flat(cmat, 2 * nbasis + 1, 2)

    def rp_copy(f):
        return remote(near[f].at[REACH], near[f].at[REACH - sigma], rp_sem, f, partner)

    def ru_copy(f):
        return remote(near[f].at[REACH], near[f].at[REACH - 2 * sigma], ru_sem, f, ahead)

    def rd_copy(f):
        return remote(near[f].at[REACH], near[f].at[REACH + 2 * sigma], rd_sem, f, behind)

    def relay_copy(f):
        return remote(near[f].at[REACH + 2 * sigma], near[f].at[REACH + sigma], relay_sem, f, partner)

    for copy in late:
        copy.wait()

    def residual(f):
        d_copy(f).wait_recv()
        q_copy(f).wait_recv()

        def rows_of(rows):
            pred = own[f, rows, :].astype(F32) + recv_p[f, 0, rows, :].astype(F32)
            pred = pred + recv_d[f, rows, :].astype(F32) + recv_q[f, rows, :].astype(F32)
            res = ivar[f, rows, :].astype(F32) * (obs[f, rows, :].astype(F32) - pred)
            near[f][REACH, rows, :] = res.astype(BF16)

        over_rows(rows_of)
        ru_copy(f).start()
        rd_copy(f).start()
        rp_copy(f).start()

    def own_prior(f):
        prec = [ftab[f_p + f * 6 + g] for g in range(filters)]

        def rows_of(rows):
            sc = scale[f, rows, :]
            pri, dev = [], []
            for which in range(2):
                total = None
                for g in range(filters):
                    sam = mean[g, rows, :] + scale[g, rows, :] * noise[which, g, rows, :].astype(F32)
                    total = prec[g] * sam if total is None else total + prec[g] * sam
                pri.append(total)
                dev.append(sc * noise[which, f, rows, :].astype(F32))
            pri_mu[f, rows, :] = 0.5 * (pri[0] + pri[1])
            pri_rho[f, rows, :] = 1.0 - 0.5 * (pri[0] * dev[0] + pri[1] * dev[1])

        over_rows(rows_of)

    def backward(f):
        ru_copy(f).wait_recv()
        rp_copy(f).wait_recv()
        relay_copy(f).wait_recv()

        def pull(q, carry):
            fq = f * K + q
            oy = itab[i_oy + fq]
            ox = itab[i_ox + fq]
            part = dot(shift_matrix(-oy), near[f][itab[i_e + fq]]).astype(BF16)
            moved[q] = dot(part, shift_matrix(ox))
            return carry

        lax.fori_loop(0, K, pull, 0)

        def adjoint(k, carry):
            coef = [
                [ftab[f_a + ((f * K + q) * nbasis + k) * 3 + m] for m in range(3)] for q in range(K)
            ]
            beta = [coef[q][2] * lcol for q in range(K)]

            def weigh_rows(rows):
                li = lrow[rows, :]
                alpha = [coef[q][0] + coef[q][1] * li for q in range(K)]
                for lo in (0, 128):
                    acc = None
                    for q in range(K):
                        term = (alpha[q] + beta[q][:, lo : lo + 128]) * moved[q, rows, lo : lo + 128]
                        acc = term if acc is None else acc + term
                    x_ref[rows, lo : lo + 128] = acc.astype(BF16)

            over_rows(weigh_rows)
            at = pl.ds(pl.multiple_of(k * side, side), side)
            half[:, at] = dot(rmat_t[k], x_ref[...]).astype(BF16)
            return carry

        lax.fori_loop(0, nbasis, adjoint, 0)
        prec = [ftab[f_p + f * 6 + filters + g] for g in range(filters)]

        def finish_rows(rows):
            grad = dot(half[rows, :], cmat[...])
            for g in range(filters):
                grad = grad - prec[g] * recv_g[g, rows, :].astype(F32)
            e_ref[s, f, rows, :] = grad.astype(BF16)

        def finish(r, carry):
            finish_rows(pl.ds(pl.multiple_of(r * 128, 128), 128))
            return carry

        lax.fori_loop(0, side // 128, finish, 0)
        e_copy(f).start()

    def e_copy(f):
        return remote(e_ref.at[s, f], e_ref.at[s, f], e_sem, f, twin)

    def outs(f):
        return (
            pltpu.make_async_copy(mu.at[f], mu_hbm.at[f], out_sem.at[0, f]),
            pltpu.make_async_copy(rho.at[f], rho_hbm.at[f], out_sem.at[1, f]),
        )

    def final(f):
        e_copy(f).wait_recv()

        def rows_of(rows):
            sc = scale[f, rows, :]
            e0 = e_ref[0, f, rows, :].astype(F32)
            e1 = e_ref[1, f, rows, :].astype(F32)
            d0 = sc * noise[0, f, rows, :].astype(F32)
            d1 = sc * noise[1, f, rows, :].astype(F32)
            mu[f, rows, :] = 0.5 * (e0 + e1) - pri_mu[f, rows, :]
            rho[f, rows, :] = 0.5 * (e0 * d0 + e1 * d1) + pri_rho[f, rows, :]

        over_rows(rows_of)
        for copy in outs(f):
            copy.start()

    def relay(f):
        rd_copy(f).wait_recv()
        relay_copy(f).start()

    for f in range(filters):
        residual(f)
    relay(0)
    for f in range(filters):
        own_prior(f)
    for f in range(filters):
        g_copy(f).wait_recv()
    backward(0)
    relay(1)
    backward(1)
    final(0)
    relay(2)
    backward(2)
    final(1)
    final(2)

    noise_out.wait_send()
    for f in range(filters):
        for copy in (p_copy, d_copy, q_copy, g_copy, ru_copy, rd_copy, rp_copy, relay_copy, e_copy):
            copy(f).wait_send()
        for copy in outs(f):
            copy.wait()


def tables(intersections, counts, psf_coeffs, prior_prec, nbasis, local_filters):
    tile_here = lax.axis_index("tile")
    first = lax.axis_index("filt") * local_filters
    fields = intersections.shape[3]
    exposures = psf_coeffs.shape[0]
    side_scale = 1.0 / 128.0
    slots = lax.dynamic_slice(intersections, (tile_here, first, 0, 0), (1, local_filters, K, fields))[0]
    live_count = lax.dynamic_slice(counts, (tile_here, first), (1, local_filters))[0]
    start = jnp.clip(tile_here - REACH, 0, exposures - WINDOW)
    psf = lax.dynamic_slice(psf_coeffs, (start, first, 0, 0), (WINDOW, local_filters, NB, 3)).astype(F32)
    live = jnp.arange(K)[None, :] < live_count[:, None]
    exposure, oy, ox, kb = slots[..., 0], slots[..., 1], slots[..., 2], slots[..., 3:]
    which = jnp.where(live, exposure - start, -1)
    hit = (which[:, :, None] == jnp.arange(WINDOW)[None, None, :]).astype(F32)
    coef = jnp.sum(hit[:, :, :, None, None] * jnp.transpose(psf, (1, 0, 2, 3))[:, None], axis=2)
    shift_y = oy.astype(F32)[:, :, None] * side_scale
    shift_x = ox.astype(F32)[:, :, None] * side_scale
    c0 = coef[..., 0] + coef[..., 1] * shift_y + coef[..., 2] * shift_x
    coef = jnp.stack([c0, coef[..., 1], coef[..., 2]], -1)
    onehot = (kb[..., None] == jnp.arange(nbasis)).astype(F32)
    per_basis = jnp.sum(onehot[..., None] * coef[:, :, :, None, :], axis=2)
    place = exposure - tile_here + REACH
    wanted = live[:, :, None] & (place[:, :, None] == jnp.arange(WINDOW))
    select = jnp.min(jnp.where(wanted, jnp.arange(K)[None, :, None], K), axis=1)
    prec = lax.dynamic_slice(prior_prec, (first, 0), (local_filters, prior_prec.shape[1]))
    rolled = jnp.where(first > 0, jnp.concatenate([prec[:, local_filters:], prec[:, :local_filters]], 1), prec)
    ints = [kb, oy, ox, jnp.clip(place, 0, WINDOW - 1), select]
    floats = [coef, per_basis, rolled]
    itab = jnp.concatenate([v.reshape(-1) for v in ints]).astype(jnp.int32)
    ftab = jnp.concatenate([v.reshape(-1) for v in floats])
    return itab, ftab


def body(tiles, sky_mean, sky_log_scale, noise_draw, observed, inv_var, intersections, counts, kernels, psf_coeffs, prior_prec):
    filters, side = sky_mean.shape[1], sky_mean.shape[2]
    nbasis, _, taps = kernels.shape
    itab, ftab = tables(intersections, counts, psf_coeffs, prior_prec, nbasis, filters)
    flat = kernels.reshape(2 * nbasis, taps)
    tap_rows = jnp.pad(jnp.concatenate([flat, flat[:, ::-1]], 0), ((0, 0), (0, 128 - taps)))
    img = (side, side)
    anyspec = pl.BlockSpec(memory_space=pl.ANY)
    vmem = pltpu.VMEM
    dma = pltpu.SemaphoreType.DMA
    mu, rho = pl.pallas_call(
        functools.partial(kernel, tiles),
        out_shape=[jax.ShapeDtypeStruct((filters,) + img, F32)] * 2,
        in_specs=[
            pl.BlockSpec(memory_space=pltpu.VMEM),
            pl.BlockSpec(memory_space=pltpu.SMEM),
            pl.BlockSpec(memory_space=pltpu.SMEM),
        ]
        + [anyspec] * 5,
        out_specs=[anyspec] * 2,
        scratch_shapes=[
            vmem((filters,) + img, F32),
            vmem((filters,) + img, F32),
            vmem((2, filters) + img, BF16),
            vmem((filters,) + img, BF16),
            vmem((filters,) + img, BF16),
            vmem(img, jnp.int32),
            vmem((side, 128), F32),
            vmem((nbasis,) + img, BF16),
            vmem((nbasis,) + img, BF16),
            vmem((nbasis * side, side), BF16),
            vmem((nbasis,) + img, BF16),
            vmem(img, BF16),
            vmem((nbasis,) + img, F32),
            vmem(img, BF16),
            vmem((K + 1,) + img, BF16),
            vmem((filters,) + img, BF16),
            vmem((filters, 2) + img, BF16),
            vmem((filters, 2) + img, BF16),
            vmem((filters,) + img, BF16),
            vmem((filters,) + img, BF16),
            vmem((filters,) + img, BF16),
            vmem((filters,) + img, BF16),
            vmem((WINDOW,) + img, BF16),
            vmem((WINDOW,) + img, BF16),
            vmem((WINDOW,) + img, BF16),
            vmem((K,) + img, F32),
            vmem((side, nbasis * side), BF16),
            vmem((filters,) + img, BF16),
            vmem((filters,) + img, BF16),
            vmem((2, filters) + img, BF16),
            vmem((filters,) + img, F32),
            vmem((filters,) + img, F32),
            vmem((filters,) + img, F32),
            vmem((filters,) + img, F32),
            dma((4, filters)),
            dma((2, filters)),
            dma((2, 1)),
        ]
        + [dma((2, filters))] * 9,
        compiler_params=pltpu.CompilerParams(
            collective_id=0, has_side_effects=True, vmem_limit_bytes=48 * 1024 * 1024
        ),
    )(tap_rows, itab, ftab, sky_mean[0], sky_log_scale[0], noise_draw[0, 0], observed[0], inv_var[0])
    return mu[None], rho[None]


def solution(mesh):
    placed = (
        P("tile", "filt", None, None),
        P("tile", "filt", None, None),
        P("mc", "tile", "filt", None, None),
        P("tile", "filt", None, None),
        P("tile", "filt", None, None),
        P(),
        P(),
        P(),
        P(),
        P(),
    )
    return jax.shard_map(
        functools.partial(body, mesh.shape["tile"]),
        mesh=mesh,
        in_specs=placed,
        out_specs=(P("tile", "filt", None, None), P("tile", "filt", None, None)),
        check_vma=False,
    )
```

```python
import functools

import jax
import jax.numpy as jnp
from jax import lax
from jax.experimental import pallas as pl
from jax.experimental.pallas import tpu as pltpu
from jax.sharding import PartitionSpec as P

NB = 6
K = 3
STRIP = 16
REACH = 2
WINDOW = 2 * REACH + 1
MESH = pl.DeviceIdType.MESH
F32 = jnp.float32
BF16 = jnp.bfloat16


def dot(a, b):
    return jnp.dot(a, b, preferred_element_type=F32)


def band_rows(pat, a, side):
    half = side // 2
    start = (16 * a - 12) % half
    rolled = pltpu.roll(pat, start, 1) if start else pat
    lane = lax.broadcasted_iota(jnp.int32, rolled.shape, 1)
    zero = jnp.zeros_like(rolled)
    low = jnp.where(lane < half // 2, rolled, zero)
    high = jnp.where(lane >= half // 2, rolled, zero)
    blocks = half // 16
    if a == 0:
        return low, zero
    if a < blocks - 1:
        return rolled, zero
    if a <= blocks:
        return high, low
    if a < 2 * blocks - 1:
        return zero, rolled
    return zero, high


def kernel(
    tiles,
    kern_hbm,
    inter_hbm,
    count_hbm,
    psf_hbm,
    prec_hbm,
    mean_hbm,
    lsc_hbm,
    noise_hbm,
    obs_hbm,
    ivar_hbm,
    mu,
    rho,
    kern,
    taps,
    inter,
    count,
    psf_b,
    psf_f,
    psf,
    prec,
    basis_v,
    per_basis,
    mean,
    scale,
    noise,
    obs,
    ivar,
    lrow,
    rmat,
    rmat_t,
    cmat,
    cmat_t,
    x_ref,
    y_ref,
    half_blur,
    blur,
    turn,
    placed,
    own,
    send_p,
    recv_p,
    send_d,
    recv_d,
    send_q,
    recv_q,
    near0,
    near1,
    near2,
    moved,
    half,
    send_g,
    recv_g,
    e_ref,
    pri_mu,
    pri_rho,
    in_sem,
    tab_sem,
    noise_sem,
    p_sem,
    d_sem,
    q_sem,
    rp_sem,
    ru_sem,
    rd_sem,
    relay_sem,
    g_sem,
    e_sem,
):
    filters, side = mean.shape[0], mean.shape[1]
    nbasis = rmat_t.shape[0]
    exposures = psf.shape[3]
    near = (near0, near1, near2)
    pad = side // 2
    t = lax.axis_index("tile")
    s = lax.axis_index("mc")
    h = lax.axis_index("filt")
    first = h * filters
    sigma = 1 - 2 * lax.rem(t, 2)
    partner = {"tile": t + sigma}
    ahead = {"tile": lax.rem(t + 2 * sigma + tiles, tiles)}
    behind = {"tile": lax.rem(t - 2 * sigma + tiles, tiles)}
    twin = {"mc": 1 - s}
    across = {"filt": 1 - h, "mc": 1 - s}

    def remote(src, dst, sem, f, to):
        return pltpu.make_async_remote_copy(
            src_ref=src,
            dst_ref=dst,
            send_sem=sem.at[0, f],
            recv_sem=sem.at[1, f],
            device_id=to,
            device_id_type=MESH,
        )

    ours = pl.ds(first, filters)
    kern_in = pltpu.make_async_copy(kern_hbm, kern, tab_sem.at[0])
    psf_in = pltpu.make_async_copy(psf_hbm.at[ours], psf_b, tab_sem.at[1])
    inter_in = pltpu.make_async_copy(inter_hbm.at[ours], inter, tab_sem.at[2])
    count_in = pltpu.make_async_copy(count_hbm, count, tab_sem.at[3])
    prec_in = pltpu.make_async_copy(prec_hbm, prec, tab_sem.at[4])
    basis_move = pltpu.make_async_copy(basis_v, per_basis, tab_sem.at[6])
    psf_move = pltpu.make_async_copy(psf_f, psf, tab_sem.at[5])
    for copy in (kern_in, psf_in, inter_in, count_in, prec_in):
        copy.start()
    loads = []
    for f in range(filters):
        loads.append(
            [
                pltpu.make_async_copy(noise_hbm.at[f], noise.at[s, f], in_sem.at[0, f]),
                pltpu.make_async_copy(mean_hbm.at[f], mean.at[f], in_sem.at[1, f]),
                pltpu.make_async_copy(lsc_hbm.at[f], scale.at[f], in_sem.at[2, f]),
            ]
        )
    late = [
        pltpu.make_async_copy(obs_hbm, obs, in_sem.at[3, 0]),
        pltpu.make_async_copy(ivar_hbm, ivar, in_sem.at[3, 1]),
    ]
    for group in loads:
        for copy in group:
            copy.start()
    for copy in late:
        copy.start()

    barrier = pltpu.get_barrier_semaphore()
    for to in (partner, ahead, behind, twin, across):
        pl.semaphore_signal(barrier, inc=1, device_id=to, device_id_type=MESH)

    centre_i = lax.broadcasted_iota(jnp.int32, (STRIP, 128), 0)
    lrow[...] = (2 * centre_i + 1 - side).astype(F32) * (1.0 / side)
    centre_j = lax.broadcasted_iota(jnp.int32, (1, side), 1)
    lcol = (2 * centre_j + 1 - side).astype(F32) * (1.0 / side)
    lanes = lax.broadcasted_iota(jnp.int32, (1, 128), 1)
    placed[K] = jnp.zeros((side, side), BF16)
    edge = jnp.zeros((pad, 128), F32)

    def clear_edges(ref, at):
        for lo in range(2):
            ref[at, lo, 0:pad, :] = edge
            ref[at, lo, pad + side : side + 2 * pad, :] = edge

    for q in range(K):
        clear_edges(turn, q)

    kern_in.wait()
    taps[...] = jnp.zeros_like(taps)
    ntaps = kern.shape[2]
    for k in range(nbasis):
        taps[2 * k : 2 * k + 2, 0:ntaps] = kern[k]
    swap_i = lax.broadcasted_iota(jnp.int32, (128, 128), 0)
    swap_j = lax.broadcasted_iota(jnp.int32, (128, 128), 1)
    swap = jnp.where(swap_i + swap_j == ntaps - 1, 1.0, 0.0).astype(BF16)
    taps[2 * nbasis : 4 * nbasis, :] = dot(taps[0 : 2 * nbasis, :].astype(BF16), swap)

    def build(dst, from_row, stride, flat):
        def one(k, carry):
            row = taps[pl.ds(from_row + stride * k, 1), :]
            pat = jnp.broadcast_to(row, (16, 128))
            pat = pltpu.roll(pat, 0, 1, stride=1, stride_axis=0)
            for a in range(side // 16):
                left, right = band_rows(pat, a, side)
                for part, lo in ((left, 0), (right, 128)):
                    if flat:
                        at = pl.ds(pl.multiple_of(k * side + 16 * a, 16), 16)
                        dst[at, lo : lo + 128] = part.astype(BF16)
                    else:
                        dst[k, 16 * a : 16 * a + 16, lo : lo + 128] = part.astype(BF16)
            return carry

        lax.fori_loop(0, nbasis, one, 0)

    build(rmat, 2 * nbasis, 2, True)
    build(cmat_t, 1, 2, False)
    psf_in.wait()
    psf_f[...] = psf_b[...].astype(F32)
    psf_move.start()

    for f in range(filters):
        loads[f][0].wait()
    pl.semaphore_wait(barrier, 5)
    noise_out = remote(noise.at[s], noise.at[s], noise_sem, 0, twin)
    noise_out.start()

    def over_rows(body, chunk=32):
        def one(r, carry):
            body(pl.multiple_of(r * chunk, chunk), chunk)
            return carry

        lax.fori_loop(0, side // chunk, one, 0)

    inter_in.wait()
    count_in.wait()
    prec_in.wait()
    psf_move.wait()

    def slot_live(f, q):
        return q < count[first + f, t]

    def slot_exposure(f, q):
        return jnp.clip(inter[f, 0, q, t], 0, exposures - 1)

    def slot_coef(f, q):
        live = slot_live(f, q)
        e = slot_exposure(f, q)
        return [[jnp.where(live, psf[f, b, m, e], 0.0) for m in range(3)] for b in range(NB)]

    def lane_shift(by):
        whole = jnp.right_shift(by, 7)
        rest = jnp.bitwise_and(by, 127)
        right = lanes >= rest
        same = ((whole == 0) & right) | ((whole == -1) & ~right)
        from_high = (whole == -1) & right
        from_low = ((whole == 0) & ~right) | (whole == 1)

        def apply(low, high):
            low = pltpu.roll(low, rest, 1)
            high = pltpu.roll(high, rest, 1)
            none = jnp.zeros_like(low)
            return (
                jnp.where(same, low, jnp.where(from_high, high, none)),
                jnp.where(same, high, jnp.where(from_low, low, none)),
            )

        return apply

    def first_weight(constant, coef, lo):
        return (constant + coef[1] * lrow[...]) + coef[2] * lcol[:, 128 * lo : 128 * lo + 128]

    def forward(f):
        def sample_rows(r, n):
            rows = pl.ds(r, n)
            sc = jnp.exp(scale[f, rows, :])
            scale[f, rows, :] = sc
            x_ref[rows, :] = (mean[f, rows, :] + sc * noise[s, f, rows, :].astype(F32)).astype(BF16)

        over_rows(sample_rows)

        half_blur[...] = dot(rmat[...], x_ref[...]).astype(BF16)
        for k in range(nbasis):
            image = dot(half_blur[k * side : (k + 1) * side, :], cmat_t[k])
            blur[k, 0] = image[:, 0:128]
            blur[k, 1] = image[:, 128:256]

        def slot(q, carry):
            coef = slot_coef(f, q)
            oy = inter[f, 1, q, t]
            ox = inter[f, 2, q, t]
            kb = [inter[f, 3 + b, q, t] for b in range(NB)]
            up = oy.astype(F32) * (2.0 / side)
            over = ox.astype(F32) * (2.0 / side)
            c0 = [coef[b][0] + coef[b][1] * up + coef[b][2] * over for b in range(NB)]
            weight = [[first_weight(c0[b], coef[b], lo) for lo in range(2)] for b in range(NB)]
            step = [coef[b][1] * (2.0 * STRIP / side) for b in range(NB)]
            move = lane_shift(ox)

            def mix_rows(i, weight):
                r = pl.multiple_of(i * STRIP, STRIP)
                for lo in range(2):
                    acc = None
                    for b in range(NB):
                        term = weight[b][lo] * blur[kb[b], lo, pl.ds(r, STRIP), :]
                        acc = term if acc is None else acc + term
                    turn[q, lo, pl.ds(pad + r, STRIP), :] = acc
                return [[weight[b][lo] + step[b] for lo in range(2)] for b in range(NB)]

            lax.fori_loop(0, side // STRIP, mix_rows, weight, unroll=4)

            def place_rows(r, n):
                low, high = move(*[turn[q, lo, pl.ds(pad - oy + r, n), :] for lo in range(2)])
                placed[q, pl.ds(r, n), 0:128] = low.astype(BF16)
                placed[q, pl.ds(r, n), 128:256] = high.astype(BF16)

            over_rows(place_rows, 64)
            return carry

        lax.fori_loop(0, K, slot, 0)
        place = [jnp.where(slot_live(f, q), inter[f, 0, q, t] - t, WINDOW) for q in range(K)]

        def pick(d):
            at = K
            for q in range(K):
                at = jnp.where(place[q] == d, q, at)
            return placed[at]

        own[f] = pick(0)
        send_p[f, 0] = pick(sigma)
        send_p[f, 1] = pick(-sigma)
        send_d[f] = pick(-2 * sigma)
        send_q[f] = pick(2 * sigma)

    def p_copy(f):
        return remote(send_p.at[f], recv_p.at[f], p_sem, f, partner)

    def d_copy(f):
        return remote(send_d.at[f], recv_d.at[f], d_sem, f, behind)

    def q_copy(f):
        return remote(send_q.at[f], recv_q.at[f], q_sem, f, ahead)

    def merge(f):
        p_copy(f).wait_recv()

        def rows_of(r, n):
            rows = pl.ds(r, n)
            joined = send_q[f, rows, :].astype(F32) + recv_p[f, 1, rows, :].astype(F32)
            send_q[f, rows, :] = joined.astype(BF16)

        over_rows(rows_of)
        q_copy(f).start()

    for f in range(filters):
        loads[f][1].wait()
        loads[f][2].wait()
        forward(f)
        p_copy(f).start()
        d_copy(f).start()
        if f > 0:
            merge(f - 1)
    merge(filters - 1)

    noise_out.wait_recv()

    def g_copy(f):
        return remote(send_g.at[f], recv_g.at[f], g_sem, f, across)

    for f in range(filters):

        def twin_rows(r, n):
            rows = pl.ds(r, n)
            other = noise[1 - s, f, rows, :].astype(F32)
            send_g[f, rows, :] = (mean[f, rows, :] + scale[f, rows, :] * other).astype(BF16)

        over_rows(twin_rows)
        g_copy(f).start()

    build(rmat_t, 0, 2, False)
    build(cmat, 2 * nbasis + 1, 2, True)

    def rp_copy(f):
        return remote(near[f].at[REACH], near[f].at[REACH - sigma], rp_sem, f, partner)

    def ru_copy(f):
        return remote(near[f].at[REACH], near[f].at[REACH - 2 * sigma], ru_sem, f, ahead)

    def rd_copy(f):
        return remote(near[f].at[REACH], near[f].at[REACH + 2 * sigma], rd_sem, f, behind)

    def relay_copy(f):
        return remote(near[f].at[REACH + 2 * sigma], near[f].at[REACH + sigma], relay_sem, f, partner)

    for copy in late:
        copy.wait()

    def residual(f):
        d_copy(f).wait_recv()
        q_copy(f).wait_recv()

        def rows_of(r, n):
            rows = pl.ds(r, n)
            pred = own[f, rows, :].astype(F32) + recv_p[f, 0, rows, :].astype(F32)
            pred = pred + recv_d[f, rows, :].astype(F32) + recv_q[f, rows, :].astype(F32)
            res = ivar[f, rows, :].astype(F32) * (obs[f, rows, :].astype(F32) - pred)
            near[f][REACH, rows, :] = res.astype(BF16)

        over_rows(rows_of)
        ru_copy(f).start()
        rd_copy(f).start()
        rp_copy(f).start()

    def basis_table(fq, carry):
        f = fq // K
        q = fq - K * f
        coef = slot_coef(f, q)
        up = inter[f, 1, q, t].astype(F32) * (2.0 / side)
        across_by = inter[f, 2, q, t].astype(F32) * (2.0 / side)
        kb = [inter[f, 3 + b, q, t] for b in range(NB)]
        for b in range(NB):
            coef[b][0] = coef[b][0] + coef[b][1] * up + coef[b][2] * across_by
        for m in range(3):
            total = jnp.zeros((1, 128), F32)
            for b in range(NB):
                total = total + jnp.where(lanes == kb[b], coef[b][m], 0.0)
            basis_v[pl.ds(3 * fq + m, 1), :] = total
        return carry

    def own_prior():
        rows_in = [[prec[first + f, first + g] for g in range(filters)] for f in range(filters)]

        def rows_of(r, n):
            rows = pl.ds(r, n)
            sam = [[None] * filters for _ in range(2)]
            dev = [[None] * filters for _ in range(2)]
            for g in range(filters):
                mn, sc = mean[g, rows, :], scale[g, rows, :]
                for which in range(2):
                    dev[which][g] = sc * noise[which, g, rows, :].astype(F32)
                    sam[which][g] = mn + dev[which][g]
            for f in range(filters):
                pri = []
                for which in range(2):
                    total = None
                    for g in range(filters):
                        term = rows_in[f][g] * sam[which][g]
                        total = term if total is None else total + term
                    pri.append(total)
                pri_mu[f, rows, :] = pri[0] + pri[1]
                pri_rho[f, rows, :] = pri[0] * dev[0][f] + pri[1] * dev[1][f]

        over_rows(rows_of, 16)

    def e_copy(f):
        return remote(e_ref.at[s, f], e_ref.at[s, f], e_sem, f, twin)

    def backward(f):
        ru_copy(f).wait_recv()
        rp_copy(f).wait_recv()
        relay_copy(f).wait_recv()

        def pull(q, carry):
            at = jnp.clip(inter[f, 0, q, t] - t + REACH, 0, WINDOW - 1)
            move = lane_shift(-inter[f, 2, q, t])

            def pull_rows(r, n):
                image = near[f][at, pl.ds(r, n), :].astype(F32)
                low, high = move(image[:, 0:128], image[:, 128:256])
                turn[q, 0, pl.ds(pad + r, n), :] = low
                turn[q, 1, pl.ds(pad + r, n), :] = high

            over_rows(pull_rows, 64)
            oy = inter[f, 1, q, t]

            def settle_rows(r, n):
                for lo in range(2):
                    moved[q, lo, pl.ds(r, n), :] = turn[q, lo, pl.ds(pad + oy + r, n), :]

            over_rows(settle_rows, 64)
            return carry

        lax.fori_loop(0, K, pull, 0)

        def weigh(k, dst):
            coef = [[per_basis[(f * K + q) * 3 + m, k] for m in range(3)] for q in range(K)]
            weight = [[first_weight(coef[q][0], coef[q], lo) for lo in range(2)] for q in range(K)]
            step = [coef[q][1] * (2.0 * STRIP / side) for q in range(K)]
            for r in range(0, side, STRIP):
                for lo in range(2):
                    acc = None
                    for q in range(K):
                        term = weight[q][lo] * moved[q, lo, r : r + STRIP, :]
                        acc = term if acc is None else acc + term
                        if r + STRIP < side:
                            weight[q][lo] = weight[q][lo] + step[q]
                    dst[r : r + STRIP, 128 * lo : 128 * lo + 128] = acc.astype(BF16)

        def pull_back(k, src):
            at = pl.ds(pl.multiple_of(k * side, side), side)
            half[:, at] = dot(rmat_t[k], src[...]).astype(BF16)

        weigh(0, x_ref)

        def pair(j, carry):
            weigh(2 * j + 1, y_ref)
            pull_back(2 * j, x_ref)
            weigh(2 * j + 2, x_ref)
            pull_back(2 * j + 1, y_ref)
            return carry

        lax.fori_loop(0, nbasis // 2 - 1, pair, 0)
        weigh(nbasis - 1, y_ref)
        pull_back(nbasis - 2, x_ref)
        pull_back(nbasis - 1, y_ref)
        others = (1 - h) * filters
        cross = [prec[first + f, others + g] for g in range(filters)]
        grad = dot(half[...], cmat[...])
        for g in range(filters):
            grad = grad - cross[g] * recv_g[g].astype(F32)
        e_ref[s, f] = grad.astype(BF16)
        e_copy(f).start()

    def final(f):
        e_copy(f).wait_recv()

        def rows_of(r, n):
            rows = pl.ds(r, n)
            sc = scale[f, rows, :]
            e0 = e_ref[0, f, rows, :].astype(F32)
            e1 = e_ref[1, f, rows, :].astype(F32)
            d0 = sc * noise[0, f, rows, :].astype(F32)
            d1 = sc * noise[1, f, rows, :].astype(F32)
            mu[f, rows, :] = 0.5 * ((e0 + e1) - pri_mu[f, rows, :])
            rho[f, rows, :] = 0.5 * ((e0 * d0 + e1 * d1) - pri_rho[f, rows, :]) + 1.0

        over_rows(rows_of)

    def relay(f):
        rd_copy(f).wait_recv()
        relay_copy(f).start()

    residual(0)
    lax.fori_loop(0, filters * K, basis_table, 0)
    basis_move.start()
    residual(1)
    own_prior()
    residual(2)
    basis_move.wait()
    relay(0)
    for f in range(filters):
        g_copy(f).wait_recv()
    backward(0)
    relay(1)
    backward(1)
    final(0)
    relay(2)
    backward(2)
    final(1)
    final(2)

    noise_out.wait_send()
    for f in range(filters):
        for copy in (p_copy, d_copy, q_copy, g_copy, ru_copy, rd_copy, rp_copy, relay_copy, e_copy):
            copy(f).wait_send()


def body(tiles, sky_mean, sky_log_scale, noise_draw, observed, inv_var, intersections, counts, kernels, psf_coeffs, prior_prec):
    filters, side = sky_mean.shape[1], sky_mean.shape[2]
    nbasis, _, taps = kernels.shape
    every, fields = intersections.shape[1], intersections.shape[3]
    exposures = psf_coeffs.shape[0]
    img = (side, side)
    padded = (2, 2 * side, 128)
    vmem = pltpu.VMEM
    smem = pltpu.SMEM
    dma = pltpu.SemaphoreType.DMA
    mu, rho = pl.pallas_call(
        functools.partial(kernel, tiles),
        out_shape=[jax.ShapeDtypeStruct((filters,) + img, F32)] * 2,
        in_specs=[pl.BlockSpec(memory_space=pltpu.HBM)] * 10,
        out_specs=[pl.BlockSpec(memory_space=pltpu.VMEM)] * 2,
        scratch_shapes=[
            vmem((nbasis, 2, taps), F32),
            vmem((4 * nbasis, 128), F32),
            smem((filters, fields, K, intersections.shape[0]), jnp.int32),
            smem((every, counts.shape[0]), jnp.int32),
            vmem((filters, NB, 3, exposures), BF16),
            vmem((filters, NB, 3, exposures), F32),
            smem((filters, NB, 3, exposures), F32),
            smem((every, every), F32),
            vmem((filters * K * 3, 128), F32),
            smem((filters * K * 3, 128), F32),
            vmem((filters,) + img, F32),
            vmem((filters,) + img, F32),
            vmem((2, filters) + img, BF16),
            vmem((filters,) + img, BF16),
            vmem((filters,) + img, BF16),
            vmem((STRIP, 128), F32),
            vmem((nbasis * side, side), BF16),
            vmem((nbasis,) + img, BF16),
            vmem((nbasis * side, side), BF16),
            vmem((nbasis,) + img, BF16),
            vmem(img, BF16),
            vmem(img, BF16),
            vmem((nbasis * side, side), BF16),
            vmem((nbasis, 2, side, 128), F32),
            vmem((K,) + padded, F32),
            vmem((K + 1,) + img, BF16),
            vmem((filters,) + img, BF16),
            vmem((filters, 2) + img, BF16),
            vmem((filters, 2) + img, BF16),
            vmem((filters,) + img, BF16),
            vmem((filters,) + img, BF16),
            vmem((filters,) + img, BF16),
            vmem((filters,) + img, BF16),
            vmem((WINDOW,) + img, BF16),
            vmem((WINDOW,) + img, BF16),
            vmem((WINDOW,) + img, BF16),
            vmem((K, 2, side, 128), F32),
            vmem((side, nbasis * side), BF16),
            vmem((filters,) + img, BF16),
            vmem((filters,) + img, BF16),
            vmem((2, filters) + img, BF16),
            vmem((filters,) + img, F32),
            vmem((filters,) + img, F32),
            dma((4, filters)),
            dma((7,)),
            dma((2, 1)),
        ]
        + [dma((2, filters))] * 9,
        compiler_params=pltpu.CompilerParams(
            collective_id=0, has_side_effects=True, vmem_limit_bytes=60 * 1024 * 1024
        ),
    )(
        kernels,
        jnp.transpose(intersections, (1, 3, 2, 0)),
        jnp.transpose(counts),
        jnp.transpose(psf_coeffs, (1, 2, 3, 0)),
        prior_prec,
        sky_mean[0],
        sky_log_scale[0],
        noise_draw[0, 0],
        observed[0],
        inv_var[0],
    )
    return mu[None], rho[None]


def solution(mesh):
    placed = (
        P("tile", "filt", None, None),
        P("tile", "filt", None, None),
        P("mc", "tile", "filt", None, None),
        P("tile", "filt", None, None),
        P("tile", "filt", None, None),
        P(),
        P(),
        P(),
        P(),
        P(),
    )
    return jax.shard_map(
        functools.partial(body, mesh.shape["tile"]),
        mesh=mesh,
        in_specs=placed,
        out_specs=(P("tile", "filt", None, None), P("tile", "filt", None, None)),
        check_vma=False,
    )
```

```python
import functools

import jax
import jax.numpy as jnp
from jax import lax
from jax.experimental import pallas as pl
from jax.experimental.pallas import tpu as pltpu
from jax.sharding import PartitionSpec as P

NB = 6
K = 3
STRIP = 16
REACH = 2
WINDOW = 2 * REACH + 1
MESH = pl.DeviceIdType.MESH
F32 = jnp.float32
BF16 = jnp.bfloat16


def dot(a, b):
    return jnp.dot(a, b, preferred_element_type=F32)


def band_rows(pat, a, side):
    half = side // 2
    start = (16 * a - 12) % half
    rolled = pltpu.roll(pat, start, 1) if start else pat
    lane = lax.broadcasted_iota(jnp.int32, rolled.shape, 1)
    zero = jnp.zeros_like(rolled)
    low = jnp.where(lane < half // 2, rolled, zero)
    high = jnp.where(lane >= half // 2, rolled, zero)
    blocks = half // 16
    if a == 0:
        return low, zero
    if a < blocks - 1:
        return rolled, zero
    if a <= blocks:
        return high, low
    if a < 2 * blocks - 1:
        return zero, rolled
    return zero, high


def kernel(
    tiles,
    kern_hbm,
    inter_hbm,
    count_hbm,
    psf_hbm,
    prec_hbm,
    mean_hbm,
    lsc_hbm,
    noise_hbm,
    obs_hbm,
    ivar_hbm,
    mu,
    rho,
    kern,
    taps,
    inter,
    count,
    psf_b,
    psf_f,
    psf,
    prec,
    basis_v,
    per_basis,
    mean,
    scale,
    noise,
    obs,
    ivar,
    lrow,
    rmat,
    rmat_t,
    cmat,
    cmat_t,
    x_ref,
    y_ref,
    half_blur,
    blur,
    turn,
    placed,
    own,
    send_p,
    recv_p,
    send_d,
    recv_d,
    send_q,
    recv_q,
    near0,
    near1,
    near2,
    moved,
    half,
    send_g,
    recv_g,
    e_ref,
    pri_mu,
    pri_rho,
    in_sem,
    tab_sem,
    noise_sem,
    p_sem,
    d_sem,
    q_sem,
    rp_sem,
    ru_sem,
    rd_sem,
    relay_sem,
    g_sem,
    e_sem,
):
    filters, side = mean.shape[0], mean.shape[1]
    nbasis = rmat_t.shape[0]
    exposures = psf.shape[3]
    near = (near0, near1, near2)
    pad = side // 2
    t = lax.axis_index("tile")
    s = lax.axis_index("mc")
    h = lax.axis_index("filt")
    first = h * filters
    sigma = 1 - 2 * lax.rem(t, 2)
    partner = {"tile": t + sigma}
    ahead = {"tile": lax.rem(t + 2 * sigma + tiles, tiles)}
    behind = {"tile": lax.rem(t - 2 * sigma + tiles, tiles)}
    twin = {"mc": 1 - s}
    across = {"filt": 1 - h, "mc": 1 - s}

    def remote(src, dst, sem, f, to):
        return pltpu.make_async_remote_copy(
            src_ref=src,
            dst_ref=dst,
            send_sem=sem.at[0, f],
            recv_sem=sem.at[1, f],
            device_id=to,
            device_id_type=MESH,
        )

    ours = pl.ds(first, filters)
    kern_in = pltpu.make_async_copy(kern_hbm, kern, tab_sem.at[0])
    psf_in = pltpu.make_async_copy(psf_hbm.at[ours], psf_b, tab_sem.at[1])
    inter_in = pltpu.make_async_copy(inter_hbm.at[ours], inter, tab_sem.at[2])
    count_in = pltpu.make_async_copy(count_hbm, count, tab_sem.at[3])
    prec_in = pltpu.make_async_copy(prec_hbm, prec, tab_sem.at[4])
    basis_move = pltpu.make_async_copy(basis_v, per_basis, tab_sem.at[6])
    psf_move = pltpu.make_async_copy(psf_f, psf, tab_sem.at[5])
    for copy in (kern_in, psf_in, inter_in, count_in, prec_in):
        copy.start()
    loads = []
    for f in range(filters):
        loads.append(
            [
                pltpu.make_async_copy(noise_hbm.at[f], noise.at[s, f], in_sem.at[0, f]),
                pltpu.make_async_copy(mean_hbm.at[f], mean.at[f], in_sem.at[1, f]),
                pltpu.make_async_copy(lsc_hbm.at[f], scale.at[f], in_sem.at[2, f]),
            ]
        )
    late = [
        pltpu.make_async_copy(obs_hbm, obs, in_sem.at[3, 0]),
        pltpu.make_async_copy(ivar_hbm, ivar, in_sem.at[3, 1]),
    ]
    for group in loads:
        for copy in group:
            copy.start()
    for copy in late:
        copy.start()

    barrier = pltpu.get_barrier_semaphore()
    for to in (partner, ahead, behind, twin, across):
        pl.semaphore_signal(barrier, inc=1, device_id=to, device_id_type=MESH)

    centre_i = lax.broadcasted_iota(jnp.int32, (STRIP, 128), 0)
    lrow[...] = (2 * centre_i + 1 - side).astype(F32) * (1.0 / side)
    centre_j = lax.broadcasted_iota(jnp.int32, (1, side), 1)
    lcol = (2 * centre_j + 1 - side).astype(F32) * (1.0 / side)
    lanes = lax.broadcasted_iota(jnp.int32, (1, 128), 1)
    placed[K] = jnp.zeros((side, side), BF16)
    edge = jnp.zeros((pad, 128), F32)

    def clear_edges(ref, at):
        for lo in range(2):
            ref[at, lo, 0:pad, :] = edge
            ref[at, lo, pad + side : side + 2 * pad, :] = edge

    for q in range(K):
        clear_edges(turn, q)

    def noise_copy(f):
        return remote(noise.at[s, f], noise.at[s, f], noise_sem, f, twin)

    for f in range(filters):
        loads[f][0].wait()
    pl.semaphore_wait(barrier, 5)
    for f in range(filters):
        noise_copy(f).start()

    kern_in.wait()
    taps[...] = jnp.zeros_like(taps)
    ntaps = kern.shape[2]
    for k in range(nbasis):
        taps[2 * k : 2 * k + 2, 0:ntaps] = kern[k]
    swap_i = lax.broadcasted_iota(jnp.int32, (128, 128), 0)
    swap_j = lax.broadcasted_iota(jnp.int32, (128, 128), 1)
    swap = jnp.where(swap_i + swap_j == ntaps - 1, 1.0, 0.0).astype(BF16)
    taps[2 * nbasis : 4 * nbasis, :] = dot(taps[0 : 2 * nbasis, :].astype(BF16), swap)

    def build(dst, from_row, stride, flat):
        def one(k, carry):
            row = taps[pl.ds(from_row + stride * k, 1), :]
            pat = jnp.broadcast_to(row, (16, 128))
            pat = pltpu.roll(pat, 0, 1, stride=1, stride_axis=0)
            for a in range(side // 16):
                left, right = band_rows(pat, a, side)
                for part, lo in ((left, 0), (right, 128)):
                    if flat:
                        at = pl.ds(pl.multiple_of(k * side + 16 * a, 16), 16)
                        dst[at, lo : lo + 128] = part.astype(BF16)
                    else:
                        dst[k, 16 * a : 16 * a + 16, lo : lo + 128] = part.astype(BF16)
            return carry

        lax.fori_loop(0, nbasis, one, 0)

    build(rmat, 2 * nbasis, 2, True)
    build(cmat_t, 1, 2, False)
    psf_in.wait()
    psf_f[...] = psf_b[...].astype(F32)
    psf_move.start()

    def over_rows(body, chunk=32):
        def one(r, carry):
            body(pl.multiple_of(r * chunk, chunk), chunk)
            return carry

        lax.fori_loop(0, side // chunk, one, 0)

    inter_in.wait()
    count_in.wait()
    prec_in.wait()
    psf_move.wait()

    def slot_live(f, q):
        return q < count[first + f, t]

    def slot_exposure(f, q):
        return jnp.clip(inter[f, 0, q, t], 0, exposures - 1)

    def slot_coef(f, q):
        live = slot_live(f, q)
        e = slot_exposure(f, q)
        return [[jnp.where(live, psf[f, b, m, e], 0.0) for m in range(3)] for b in range(NB)]

    def lane_shift(by):
        whole = jnp.right_shift(by, 7)
        rest = jnp.bitwise_and(by, 127)
        right = lanes >= rest
        same = ((whole == 0) & right) | ((whole == -1) & ~right)
        from_high = (whole == -1) & right
        from_low = ((whole == 0) & ~right) | (whole == 1)

        def apply(low, high):
            low = pltpu.roll(low, rest, 1)
            high = pltpu.roll(high, rest, 1)
            none = jnp.zeros_like(low)
            return (
                jnp.where(same, low, jnp.where(from_high, high, none)),
                jnp.where(same, high, jnp.where(from_low, low, none)),
            )

        return apply

    def first_weight(constant, coef, lo):
        return (constant + coef[1] * lrow[...]) + coef[2] * lcol[:, 128 * lo : 128 * lo + 128]

    def forward(f):
        def sample_rows(r, n):
            rows = pl.ds(r, n)
            sc = jnp.exp(scale[f, rows, :])
            scale[f, rows, :] = sc
            x_ref[rows, :] = (mean[f, rows, :] + sc * noise[s, f, rows, :].astype(F32)).astype(BF16)

        over_rows(sample_rows)

        half_blur[...] = dot(rmat[...], x_ref[...]).astype(BF16)
        for k in range(nbasis):
            image = dot(half_blur[k * side : (k + 1) * side, :], cmat_t[k])
            blur[k, 0] = image[:, 0:128]
            blur[k, 1] = image[:, 128:256]

        def slot(q, carry):
            coef = slot_coef(f, q)
            oy = inter[f, 1, q, t]
            ox = inter[f, 2, q, t]
            kb = [inter[f, 3 + b, q, t] for b in range(NB)]
            up = oy.astype(F32) * (2.0 / side)
            over = ox.astype(F32) * (2.0 / side)
            c0 = [coef[b][0] + coef[b][1] * up + coef[b][2] * over for b in range(NB)]
            weight = [[first_weight(c0[b], coef[b], lo) for lo in range(2)] for b in range(NB)]
            step = [coef[b][1] * (2.0 * STRIP / side) for b in range(NB)]
            move = lane_shift(ox)

            def mix_rows(i, weight):
                r = pl.multiple_of(i * STRIP, STRIP)
                for lo in range(2):
                    acc = None
                    for b in range(NB):
                        term = weight[b][lo] * blur[kb[b], lo, pl.ds(r, STRIP), :]
                        acc = term if acc is None else acc + term
                    turn[q, lo, pl.ds(pad + r, STRIP), :] = acc
                return [[weight[b][lo] + step[b] for lo in range(2)] for b in range(NB)]

            lax.fori_loop(0, side // STRIP, mix_rows, weight, unroll=4)

            def place_rows(r, n):
                low, high = move(*[turn[q, lo, pl.ds(pad - oy + r, n), :] for lo in range(2)])
                placed[q, pl.ds(r, n), 0:128] = low.astype(BF16)
                placed[q, pl.ds(r, n), 128:256] = high.astype(BF16)

            over_rows(place_rows, 64)
            return carry

        lax.fori_loop(0, K, slot, 0)
        place = [jnp.where(slot_live(f, q), inter[f, 0, q, t] - t, WINDOW) for q in range(K)]

        def pick(d):
            at = K
            for q in range(K):
                at = jnp.where(place[q] == d, q, at)
            return placed[at]

        own[f] = pick(0)
        send_p[f, 0] = pick(sigma)
        send_p[f, 1] = pick(-sigma)
        send_d[f] = pick(-2 * sigma)
        send_q[f] = pick(2 * sigma)

    def p_copy(f):
        return remote(send_p.at[f], recv_p.at[f], p_sem, f, partner)

    def d_copy(f):
        return remote(send_d.at[f], recv_d.at[f], d_sem, f, behind)

    def q_copy(f):
        return remote(send_q.at[f], recv_q.at[f], q_sem, f, ahead)

    def merge(f):
        p_copy(f).wait_recv()

        def rows_of(r, n):
            rows = pl.ds(r, n)
            joined = send_q[f, rows, :].astype(F32) + recv_p[f, 1, rows, :].astype(F32)
            send_q[f, rows, :] = joined.astype(BF16)

        over_rows(rows_of)
        q_copy(f).start()

    def g_copy(f):
        return remote(send_g.at[f], recv_g.at[f], g_sem, f, across)

    def twin_sample(f):
        noise_copy(f).wait_recv()

        def twin_rows(r, n):
            rows = pl.ds(r, n)
            other = noise[1 - s, f, rows, :].astype(F32)
            send_g[f, rows, :] = (mean[f, rows, :] + scale[f, rows, :] * other).astype(BF16)

        over_rows(twin_rows)
        g_copy(f).start()

    def rp_copy(f):
        return remote(near[f].at[REACH], near[f].at[REACH - sigma], rp_sem, f, partner)

    def ru_copy(f):
        return remote(near[f].at[REACH], near[f].at[REACH - 2 * sigma], ru_sem, f, ahead)

    def rd_copy(f):
        return remote(near[f].at[REACH], near[f].at[REACH + 2 * sigma], rd_sem, f, behind)

    def relay_copy(f):
        return remote(near[f].at[REACH + 2 * sigma], near[f].at[REACH + sigma], relay_sem, f, partner)

    def residual(f):
        d_copy(f).wait_recv()
        q_copy(f).wait_recv()

        def rows_of(r, n):
            rows = pl.ds(r, n)
            pred = own[f, rows, :].astype(F32) + recv_p[f, 0, rows, :].astype(F32)
            pred = pred + recv_d[f, rows, :].astype(F32) + recv_q[f, rows, :].astype(F32)
            res = ivar[f, rows, :].astype(F32) * (obs[f, rows, :].astype(F32) - pred)
            near[f][REACH, rows, :] = res.astype(BF16)

        over_rows(rows_of)
        ru_copy(f).start()
        rd_copy(f).start()
        rp_copy(f).start()

    def basis_table(fq, carry):
        f = fq // K
        q = fq - K * f
        coef = slot_coef(f, q)
        up = inter[f, 1, q, t].astype(F32) * (2.0 / side)
        across_by = inter[f, 2, q, t].astype(F32) * (2.0 / side)
        kb = [inter[f, 3 + b, q, t] for b in range(NB)]
        for b in range(NB):
            coef[b][0] = coef[b][0] + coef[b][1] * up + coef[b][2] * across_by
        for m in range(3):
            total = jnp.zeros((1, 128), F32)
            for b in range(NB):
                total = total + jnp.where(lanes == kb[b], coef[b][m], 0.0)
            basis_v[pl.ds(3 * fq + m, 1), :] = total
        return carry

    def own_prior():
        rows_in = [[prec[first + f, first + g] for g in range(filters)] for f in range(filters)]

        def rows_of(r, n):
            rows = pl.ds(r, n)
            sam = [[None] * filters for _ in range(2)]
            dev = [[None] * filters for _ in range(2)]
            for g in range(filters):
                mn, sc = mean[g, rows, :], scale[g, rows, :]
                for which in range(2):
                    dev[which][g] = sc * noise[which, g, rows, :].astype(F32)
                    sam[which][g] = mn + dev[which][g]
            for f in range(filters):
                pri = []
                for which in range(2):
                    total = None
                    for g in range(filters):
                        term = rows_in[f][g] * sam[which][g]
                        total = term if total is None else total + term
                    pri.append(total)
                pri_mu[f, rows, :] = pri[0] + pri[1]
                pri_rho[f, rows, :] = pri[0] * dev[0][f] + pri[1] * dev[1][f]

        over_rows(rows_of, 16)

    def e_copy(f):
        return remote(e_ref.at[s, f], e_ref.at[s, f], e_sem, f, twin)

    def backward(f):
        ru_copy(f).wait_recv()
        rp_copy(f).wait_recv()
        relay_copy(f).wait_recv()

        def pull(q, carry):
            at = jnp.clip(inter[f, 0, q, t] - t + REACH, 0, WINDOW - 1)
            move = lane_shift(-inter[f, 2, q, t])

            def pull_rows(r, n):
                image = near[f][at, pl.ds(r, n), :].astype(F32)
                low, high = move(image[:, 0:128], image[:, 128:256])
                turn[q, 0, pl.ds(pad + r, n), :] = low
                turn[q, 1, pl.ds(pad + r, n), :] = high

            over_rows(pull_rows, 64)
            oy = inter[f, 1, q, t]

            def settle_rows(r, n):
                for lo in range(2):
                    moved[q, lo, pl.ds(r, n), :] = turn[q, lo, pl.ds(pad + oy + r, n), :]

            over_rows(settle_rows, 64)
            return carry

        lax.fori_loop(0, K, pull, 0)

        def weigh(k, dst):
            coef = [[per_basis[(f * K + q) * 3 + m, k] for m in range(3)] for q in range(K)]
            weight = [[first_weight(coef[q][0], coef[q], lo) for lo in range(2)] for q in range(K)]
            step = [coef[q][1] * (2.0 * STRIP / side) for q in range(K)]
            for r in range(0, side, STRIP):
                for lo in range(2):
                    acc = None
                    for q in range(K):
                        term = weight[q][lo] * moved[q, lo, r : r + STRIP, :]
                        acc = term if acc is None else acc + term
                        if r + STRIP < side:
                            weight[q][lo] = weight[q][lo] + step[q]
                    dst[r : r + STRIP, 128 * lo : 128 * lo + 128] = acc.astype(BF16)

        def pull_back(k, src):
            at = pl.ds(pl.multiple_of(k * side, side), side)
            half[:, at] = dot(rmat_t[k], src[...]).astype(BF16)

        weigh(0, x_ref)

        def pair(j, carry):
            weigh(2 * j + 1, y_ref)
            pull_back(2 * j, x_ref)
            weigh(2 * j + 2, x_ref)
            pull_back(2 * j + 1, y_ref)
            return carry

        lax.fori_loop(0, nbasis // 2 - 1, pair, 0)
        weigh(nbasis - 1, y_ref)
        pull_back(nbasis - 2, x_ref)
        pull_back(nbasis - 1, y_ref)
        if f == 0:
            for g in range(filters):
                g_copy(g).wait_recv()
        others = (1 - h) * filters
        cross = [prec[first + f, others + g] for g in range(filters)]
        grad = dot(half[...], cmat[...])
        for g in range(filters):
            grad = grad - cross[g] * recv_g[g].astype(F32)
        e_ref[s, f] = grad.astype(BF16)
        e_copy(f).start()

    def final(f):
        e_copy(f).wait_recv()

        def rows_of(r, n):
            rows = pl.ds(r, n)
            sc = scale[f, rows, :]
            e0 = e_ref[0, f, rows, :].astype(F32)
            e1 = e_ref[1, f, rows, :].astype(F32)
            d0 = sc * noise[0, f, rows, :].astype(F32)
            d1 = sc * noise[1, f, rows, :].astype(F32)
            mu[f, rows, :] = 0.5 * ((e0 + e1) - pri_mu[f, rows, :])
            rho[f, rows, :] = 0.5 * ((e0 * d0 + e1 * d1) - pri_rho[f, rows, :]) + 1.0

        over_rows(rows_of)

    def relay(f):
        rd_copy(f).wait_recv()
        relay_copy(f).start()

    def start_forward(f):
        loads[f][1].wait()
        loads[f][2].wait()
        forward(f)
        p_copy(f).start()
        d_copy(f).start()

    start_forward(0)
    start_forward(1)
    merge(0)
    twin_sample(0)
    start_forward(2)
    merge(1)
    for copy in late:
        copy.wait()
    twin_sample(1)
    merge(2)
    residual(0)
    lax.fori_loop(0, filters * K, basis_table, 0)
    basis_move.start()
    build(rmat_t, 0, 2, False)
    residual(1)
    build(cmat, 2 * nbasis + 1, 2, True)
    twin_sample(2)
    own_prior()
    residual(2)
    basis_move.wait()
    relay(0)
    backward(0)
    relay(1)
    backward(1)
    final(0)
    relay(2)
    backward(2)
    final(1)
    final(2)

    for f in range(filters):
        for copy in (noise_copy, p_copy, d_copy, q_copy, g_copy, ru_copy, rd_copy, rp_copy, relay_copy, e_copy):
            copy(f).wait_send()


def body(tiles, sky_mean, sky_log_scale, noise_draw, observed, inv_var, intersections, counts, kernels, psf_coeffs, prior_prec):
    filters, side = sky_mean.shape[1], sky_mean.shape[2]
    nbasis, _, taps = kernels.shape
    every, fields = intersections.shape[1], intersections.shape[3]
    exposures = psf_coeffs.shape[0]
    img = (side, side)
    padded = (2, 2 * side, 128)
    vmem = pltpu.VMEM
    smem = pltpu.SMEM
    dma = pltpu.SemaphoreType.DMA
    mu, rho = pl.pallas_call(
        functools.partial(kernel, tiles),
        out_shape=[jax.ShapeDtypeStruct((filters,) + img, F32)] * 2,
        in_specs=[pl.BlockSpec(memory_space=pltpu.HBM)] * 10,
        out_specs=[pl.BlockSpec(memory_space=pltpu.VMEM)] * 2,
        scratch_shapes=[
            vmem((nbasis, 2, taps), F32),
            vmem((4 * nbasis, 128), F32),
            smem((filters, fields, K, intersections.shape[0]), jnp.int32),
            smem((every, counts.shape[0]), jnp.int32),
            vmem((filters, NB, 3, exposures), BF16),
            vmem((filters, NB, 3, exposures), F32),
            smem((filters, NB, 3, exposures), F32),
            smem((every, every), F32),
            vmem((filters * K * 3, 128), F32),
            smem((filters * K * 3, 128), F32),
            vmem((filters,) + img, F32),
            vmem((filters,) + img, F32),
            vmem((2, filters) + img, BF16),
            vmem((filters,) + img, BF16),
            vmem((filters,) + img, BF16),
            vmem((STRIP, 128), F32),
            vmem((nbasis * side, side), BF16),
            vmem((nbasis,) + img, BF16),
            vmem((nbasis * side, side), BF16),
            vmem((nbasis,) + img, BF16),
            vmem(img, BF16),
            vmem(img, BF16),
            vmem((nbasis * side, side), BF16),
            vmem((nbasis, 2, side, 128), F32),
            vmem((K,) + padded, F32),
            vmem((K + 1,) + img, BF16),
            vmem((filters,) + img, BF16),
            vmem((filters, 2) + img, BF16),
            vmem((filters, 2) + img, BF16),
            vmem((filters,) + img, BF16),
            vmem((filters,) + img, BF16),
            vmem((filters,) + img, BF16),
            vmem((filters,) + img, BF16),
            vmem((WINDOW,) + img, BF16),
            vmem((WINDOW,) + img, BF16),
            vmem((WINDOW,) + img, BF16),
            vmem((K, 2, side, 128), F32),
            vmem((side, nbasis * side), BF16),
            vmem((filters,) + img, BF16),
            vmem((filters,) + img, BF16),
            vmem((2, filters) + img, BF16),
            vmem((filters,) + img, F32),
            vmem((filters,) + img, F32),
            dma((4, filters)),
            dma((7,)),
            ]
        + [dma((2, filters))] * 10,
        compiler_params=pltpu.CompilerParams(
            collective_id=0, has_side_effects=True, vmem_limit_bytes=48 * 1024 * 1024
        ),
    )(
        *[
            pltpu.with_memory_space_constraint(value, pltpu.HBM)
            for value in (
                kernels,
                jnp.transpose(intersections, (1, 3, 2, 0)),
                jnp.transpose(counts),
                jnp.transpose(psf_coeffs, (1, 2, 3, 0)),
                prior_prec,
                sky_mean[0],
                sky_log_scale[0],
                noise_draw[0, 0],
                observed[0],
                inv_var[0],
            )
        ]
    )
    return mu[None], rho[None]


def solution(mesh):
    placed = (
        P("tile", "filt", None, None),
        P("tile", "filt", None, None),
        P("mc", "tile", "filt", None, None),
        P("tile", "filt", None, None),
        P("tile", "filt", None, None),
        P(),
        P(),
        P(),
        P(),
        P(),
    )
    return jax.shard_map(
        functools.partial(body, mesh.shape["tile"]),
        mesh=mesh,
        in_specs=placed,
        out_specs=(P("tile", "filt", None, None), P("tile", "filt", None, None)),
        check_vma=False,
    )
```

```python
import functools

import jax
import jax.numpy as jnp
from jax import lax
from jax.experimental import pallas as pl
from jax.experimental.pallas import tpu as pltpu
from jax.sharding import PartitionSpec as P

NB = 6
K = 3
STRIP = 16
REACH = 2
WINDOW = 2 * REACH + 1
MESH = pl.DeviceIdType.MESH
F32 = jnp.float32
BF16 = jnp.bfloat16


def dot(a, b):
    return jnp.dot(a, b, preferred_element_type=F32)


def band_rows(pat, a, side):
    half = side // 2
    start = (16 * a - 12) % half
    rolled = pltpu.roll(pat, start, 1) if start else pat
    lane = lax.broadcasted_iota(jnp.int32, rolled.shape, 1)
    zero = jnp.zeros_like(rolled)
    low = jnp.where(lane < half // 2, rolled, zero)
    high = jnp.where(lane >= half // 2, rolled, zero)
    blocks = half // 16
    if a == 0:
        return low, zero
    if a < blocks - 1:
        return rolled, zero
    if a <= blocks:
        return high, low
    if a < 2 * blocks - 1:
        return zero, rolled
    return zero, high


def kernel(
    tiles,
    kern_hbm,
    inter_hbm,
    count_hbm,
    psf_hbm,
    prec_hbm,
    mean_hbm,
    lsc_hbm,
    noise_hbm,
    obs_hbm,
    ivar_hbm,
    mu,
    rho,
    kern,
    taps,
    inter,
    count,
    psf_b,
    psf_f,
    psf,
    prec,
    basis_v,
    per_basis,
    mean,
    scale,
    noise,
    obs,
    ivar,
    lrow,
    rmat,
    rmat_t,
    cmat,
    cmat_t,
    x_ref,
    y_ref,
    half_blur,
    blur,
    turn,
    placed,
    own,
    send_p,
    recv_p,
    send_d,
    recv_d,
    send_q,
    recv_q,
    near0,
    near1,
    near2,
    moved,
    half,
    send_g,
    recv_g,
    e_ref,
    pri_mu,
    pri_rho,
    in_sem,
    tab_sem,
    noise_sem,
    p_sem,
    d_sem,
    q_sem,
    rp_sem,
    ru_sem,
    rd_sem,
    relay_sem,
    g_sem,
    e_sem,
):
    filters, side = mean.shape[0], mean.shape[1]
    nbasis = rmat_t.shape[0]
    exposures = psf.shape[3]
    near = (near0, near1, near2)
    pad = side // 2
    t = lax.axis_index("tile")
    s = lax.axis_index("mc")
    h = lax.axis_index("filt")
    first = h * filters
    sigma = 1 - 2 * lax.rem(t, 2)
    partner = {"tile": t + sigma}
    ahead = {"tile": lax.rem(t + 2 * sigma + tiles, tiles)}
    behind = {"tile": lax.rem(t - 2 * sigma + tiles, tiles)}
    twin = {"mc": 1 - s}
    across = {"filt": 1 - h, "mc": 1 - s}

    def remote(src, dst, sem, f, to):
        return pltpu.make_async_remote_copy(
            src_ref=src,
            dst_ref=dst,
            send_sem=sem.at[0, f],
            recv_sem=sem.at[1, f],
            device_id=to,
            device_id_type=MESH,
        )

    ours = pl.ds(first, filters)
    kern_in = pltpu.make_async_copy(kern_hbm, kern, tab_sem.at[0])
    psf_in = pltpu.make_async_copy(psf_hbm.at[ours], psf_b, tab_sem.at[1])
    inter_in = pltpu.make_async_copy(inter_hbm.at[ours], inter, tab_sem.at[2])
    count_in = pltpu.make_async_copy(count_hbm, count, tab_sem.at[3])
    prec_in = pltpu.make_async_copy(prec_hbm, prec, tab_sem.at[4])
    basis_move = pltpu.make_async_copy(basis_v, per_basis, tab_sem.at[6])
    psf_move = pltpu.make_async_copy(psf_f, psf, tab_sem.at[5])
    for copy in (kern_in, psf_in, inter_in, count_in, prec_in):
        copy.start()
    loads = []
    for f in range(filters):
        loads.append(
            [
                pltpu.make_async_copy(noise_hbm.at[f], noise.at[s, f], in_sem.at[0, f]),
                pltpu.make_async_copy(mean_hbm.at[f], mean.at[f], in_sem.at[1, f]),
                pltpu.make_async_copy(lsc_hbm.at[f], scale.at[f], in_sem.at[2, f]),
            ]
        )
    late = [
        pltpu.make_async_copy(obs_hbm, obs, in_sem.at[3, 0]),
        pltpu.make_async_copy(ivar_hbm, ivar, in_sem.at[3, 1]),
    ]
    for group in loads:
        for copy in group:
            copy.start()
    for copy in late:
        copy.start()

    barrier = pltpu.get_barrier_semaphore()
    for to in (partner, ahead, behind, twin, across):
        pl.semaphore_signal(barrier, inc=1, device_id=to, device_id_type=MESH)

    centre_i = lax.broadcasted_iota(jnp.int32, (STRIP, 128), 0)
    lrow[...] = (2 * centre_i + 1 - side).astype(F32) * (1.0 / side)
    centre_j = lax.broadcasted_iota(jnp.int32, (1, side), 1)
    lcol = (2 * centre_j + 1 - side).astype(F32) * (1.0 / side)
    lanes = lax.broadcasted_iota(jnp.int32, (1, 128), 1)
    placed[K] = jnp.zeros((side, side), BF16)
    edge = jnp.zeros((pad, 128), F32)

    def clear_edges(ref, at):
        for lo in range(2):
            ref[at, lo, 0:pad, :] = edge
            ref[at, lo, pad + side : side + 2 * pad, :] = edge

    for q in range(K):
        clear_edges(turn, q)

    def noise_copy(f):
        return remote(noise.at[s, f], noise.at[s, f], noise_sem, f, twin)

    for f in range(filters):
        loads[f][0].wait()
    pl.semaphore_wait(barrier, 5)
    for f in range(filters):
        noise_copy(f).start()

    kern_in.wait()
    taps[...] = jnp.zeros_like(taps)
    ntaps = kern.shape[2]
    for k in range(nbasis):
        taps[2 * k : 2 * k + 2, 0:ntaps] = kern[k]
    swap_i = lax.broadcasted_iota(jnp.int32, (128, 128), 0)
    swap_j = lax.broadcasted_iota(jnp.int32, (128, 128), 1)
    swap = jnp.where(swap_i + swap_j == ntaps - 1, 1.0, 0.0).astype(BF16)
    taps[2 * nbasis : 4 * nbasis, :] = dot(taps[0 : 2 * nbasis, :].astype(BF16), swap)

    def build(dst, from_row, stride, flat):
        def one(k, carry):
            row = taps[pl.ds(from_row + stride * k, 1), :]
            pat = jnp.broadcast_to(row, (16, 128))
            pat = pltpu.roll(pat, 0, 1, stride=1, stride_axis=0)
            for a in range(side // 16):
                left, right = band_rows(pat, a, side)
                for part, lo in ((left, 0), (right, 128)):
                    if flat:
                        at = pl.ds(pl.multiple_of(k * side + 16 * a, 16), 16)
                        dst[at, lo : lo + 128] = part.astype(BF16)
                    else:
                        dst[k, 16 * a : 16 * a + 16, lo : lo + 128] = part.astype(BF16)
            return carry

        lax.fori_loop(0, nbasis, one, 0)

    build(rmat, 2 * nbasis, 2, True)
    build(cmat_t, 1, 2, False)
    psf_in.wait()
    psf_f[...] = psf_b[...].astype(F32)
    psf_move.start()

    def over_rows(body, chunk=32):
        for r in range(0, side, chunk):
            body(r, chunk)

    inter_in.wait()
    count_in.wait()
    prec_in.wait()
    psf_move.wait()

    def slot_live(f, q):
        return q < count[first + f, t]

    def slot_exposure(f, q):
        return jnp.clip(inter[f, 0, q, t], 0, exposures - 1)

    def slot_coef(f, q):
        live = slot_live(f, q)
        e = slot_exposure(f, q)
        return [[jnp.where(live, psf[f, b, m, e], 0.0) for m in range(3)] for b in range(NB)]

    def lane_shift(by):
        whole = jnp.right_shift(by, 7)
        rest = jnp.bitwise_and(by, 127)
        right = lanes >= rest
        same = ((whole == 0) & right) | ((whole == -1) & ~right)
        from_high = (whole == -1) & right
        from_low = ((whole == 0) & ~right) | (whole == 1)

        def apply(low, high):
            low = pltpu.roll(low, rest, 1)
            high = pltpu.roll(high, rest, 1)
            none = jnp.zeros_like(low)
            return (
                jnp.where(same, low, jnp.where(from_high, high, none)),
                jnp.where(same, high, jnp.where(from_low, low, none)),
            )

        return apply

    def first_weight(constant, coef, lo):
        return (constant + coef[1] * lrow[...]) + coef[2] * lcol[:, 128 * lo : 128 * lo + 128]

    def forward(f, between):
        def sample_rows(r, n):
            rows = pl.ds(r, n)
            sc = jnp.exp(scale[f, rows, :])
            scale[f, rows, :] = sc
            x_ref[rows, :] = (mean[f, rows, :] + sc * noise[s, f, rows, :].astype(F32)).astype(BF16)

        over_rows(sample_rows)

        half_blur[...] = dot(rmat[...], x_ref[...]).astype(BF16)
        for k in range(nbasis):
            image = dot(half_blur[k * side : (k + 1) * side, :], cmat_t[k])
            blur[k, 0] = image[:, 0:128]
            blur[k, 1] = image[:, 128:256]

        between()

        def slot(q, carry):
            coef = slot_coef(f, q)
            oy = inter[f, 1, q, t]
            ox = inter[f, 2, q, t]
            kb = [inter[f, 3 + b, q, t] for b in range(NB)]
            up = oy.astype(F32) * (2.0 / side)
            over = ox.astype(F32) * (2.0 / side)
            c0 = [coef[b][0] + coef[b][1] * up + coef[b][2] * over for b in range(NB)]
            weight = [[first_weight(c0[b], coef[b], lo) for lo in range(2)] for b in range(NB)]
            step = [coef[b][1] * (2.0 * STRIP / side) for b in range(NB)]
            move = lane_shift(ox)

            def mix_rows(i, weight):
                r = i * STRIP
                for lo in range(2):
                    acc = None
                    for b in range(NB):
                        term = weight[b][lo] * blur[kb[b], lo, pl.ds(r, STRIP), :]
                        acc = term if acc is None else acc + term
                    turn[q, lo, pl.ds(pad + r, STRIP), :] = acc
                return [[weight[b][lo] + step[b] for lo in range(2)] for b in range(NB)]

            for i in range(side // STRIP):
                weight = mix_rows(i, weight)

            def place_rows(r, n):
                low, high = move(*[turn[q, lo, pl.ds(pad - oy + r, n), :] for lo in range(2)])
                placed[q, pl.ds(r, n), 0:128] = low.astype(BF16)
                placed[q, pl.ds(r, n), 128:256] = high.astype(BF16)

            for r in range(0, side, 64):
                place_rows(r, 64)
            return carry

        for q in range(K):
            slot(q, 0)
        place = [jnp.where(slot_live(f, q), inter[f, 0, q, t] - t, WINDOW) for q in range(K)]

        def pick(d):
            at = K
            for q in range(K):
                at = jnp.where(place[q] == d, q, at)
            return placed[at]

        own[f] = pick(0)
        send_p[f, 0] = pick(sigma)
        send_p[f, 1] = pick(-sigma)
        send_d[f] = pick(-2 * sigma)
        send_q[f] = pick(2 * sigma)

    def p_copy(f):
        return remote(send_p.at[f], recv_p.at[f], p_sem, f, partner)

    def d_copy(f):
        return remote(send_d.at[f], recv_d.at[f], d_sem, f, behind)

    def q_copy(f):
        return remote(send_q.at[f], recv_q.at[f], q_sem, f, ahead)

    def merge(f):
        p_copy(f).wait_recv()

        def rows_of(r, n):
            rows = pl.ds(r, n)
            joined = send_q[f, rows, :].astype(F32) + recv_p[f, 1, rows, :].astype(F32)
            send_q[f, rows, :] = joined.astype(BF16)

        over_rows(rows_of)
        q_copy(f).start()

    def g_copy(f):
        return remote(send_g.at[f], recv_g.at[f], g_sem, f, across)

    def twin_sample(f):
        noise_copy(f).wait_recv()

        def twin_rows(r, n):
            rows = pl.ds(r, n)
            other = noise[1 - s, f, rows, :].astype(F32)
            send_g[f, rows, :] = (mean[f, rows, :] + scale[f, rows, :] * other).astype(BF16)

        over_rows(twin_rows)
        g_copy(f).start()

    def rp_copy(f):
        return remote(near[f].at[REACH], near[f].at[REACH - sigma], rp_sem, f, partner)

    def ru_copy(f):
        return remote(near[f].at[REACH], near[f].at[REACH - 2 * sigma], ru_sem, f, ahead)

    def rd_copy(f):
        return remote(near[f].at[REACH], near[f].at[REACH + 2 * sigma], rd_sem, f, behind)

    def relay_copy(f):
        return remote(near[f].at[REACH + 2 * sigma], near[f].at[REACH + sigma], relay_sem, f, partner)

    def residual(f):
        d_copy(f).wait_recv()
        q_copy(f).wait_recv()

        def rows_of(r, n):
            rows = pl.ds(r, n)
            pred = own[f, rows, :].astype(F32) + recv_p[f, 0, rows, :].astype(F32)
            pred = pred + recv_d[f, rows, :].astype(F32) + recv_q[f, rows, :].astype(F32)
            res = ivar[f, rows, :].astype(F32) * (obs[f, rows, :].astype(F32) - pred)
            near[f][REACH, rows, :] = res.astype(BF16)

        over_rows(rows_of)
        ru_copy(f).start()
        rd_copy(f).start()
        rp_copy(f).start()

    def basis_table(fq, carry):
        f = fq // K
        q = fq - K * f
        coef = slot_coef(f, q)
        up = inter[f, 1, q, t].astype(F32) * (2.0 / side)
        across_by = inter[f, 2, q, t].astype(F32) * (2.0 / side)
        kb = [inter[f, 3 + b, q, t] for b in range(NB)]
        for b in range(NB):
            coef[b][0] = coef[b][0] + coef[b][1] * up + coef[b][2] * across_by
        for m in range(3):
            total = jnp.zeros((1, 128), F32)
            for b in range(NB):
                total = total + jnp.where(lanes == kb[b], coef[b][m], 0.0)
            basis_v[pl.ds(3 * fq + m, 1), :] = total
        return carry

    def own_prior():
        rows_in = [[prec[first + f, first + g] for g in range(filters)] for f in range(filters)]

        def rows_of(r, n):
            rows = pl.ds(r, n)
            sam = [[None] * filters for _ in range(2)]
            dev = [[None] * filters for _ in range(2)]
            for g in range(filters):
                mn, sc = mean[g, rows, :], scale[g, rows, :]
                for which in range(2):
                    dev[which][g] = sc * noise[which, g, rows, :].astype(F32)
                    sam[which][g] = mn + dev[which][g]
            for f in range(filters):
                pri = []
                for which in range(2):
                    total = None
                    for g in range(filters):
                        term = rows_in[f][g] * sam[which][g]
                        total = term if total is None else total + term
                    pri.append(total)
                pri_mu[f, rows, :] = pri[0] + pri[1]
                pri_rho[f, rows, :] = pri[0] * dev[0][f] + pri[1] * dev[1][f]

        over_rows(rows_of, 16)

    def e_copy(f):
        return remote(e_ref.at[s, f], e_ref.at[s, f], e_sem, f, twin)

    def backward(f, between):
        ru_copy(f).wait_recv()
        rp_copy(f).wait_recv()
        relay_copy(f).wait_recv()

        def pull(q, carry):
            at = jnp.clip(inter[f, 0, q, t] - t + REACH, 0, WINDOW - 1)
            move = lane_shift(-inter[f, 2, q, t])

            def pull_rows(r, n):
                image = near[f][at, pl.ds(r, n), :].astype(F32)
                low, high = move(image[:, 0:128], image[:, 128:256])
                turn[q, 0, pl.ds(pad + r, n), :] = low
                turn[q, 1, pl.ds(pad + r, n), :] = high

            over_rows(pull_rows, 64)
            oy = inter[f, 1, q, t]

            def settle_rows(r, n):
                for lo in range(2):
                    moved[q, lo, pl.ds(r, n), :] = turn[q, lo, pl.ds(pad + oy + r, n), :]

            over_rows(settle_rows, 64)
            return carry

        for q in range(K):
            pull(q, 0)

        def weigh(k, dst):
            coef = [[per_basis[(f * K + q) * 3 + m, k] for m in range(3)] for q in range(K)]
            weight = [[first_weight(coef[q][0], coef[q], lo) for lo in range(2)] for q in range(K)]
            step = [coef[q][1] * (2.0 * STRIP / side) for q in range(K)]
            for r in range(0, side, STRIP):
                for lo in range(2):
                    acc = None
                    for q in range(K):
                        term = weight[q][lo] * moved[q, lo, r : r + STRIP, :]
                        acc = term if acc is None else acc + term
                        if r + STRIP < side:
                            weight[q][lo] = weight[q][lo] + step[q]
                    dst[r : r + STRIP, 128 * lo : 128 * lo + 128] = acc.astype(BF16)

        def pull_back(k, src):
            half[:, k * side : (k + 1) * side] = dot(rmat_t[k], src[...]).astype(BF16)

        weigh(0, x_ref)

        def pair(j, carry):
            weigh(2 * j + 1, y_ref)
            pull_back(2 * j, x_ref)
            weigh(2 * j + 2, x_ref)
            pull_back(2 * j + 1, y_ref)
            return carry

        for j in range(nbasis // 2 - 1):
            pair(j, 0)
        between()
        weigh(nbasis - 1, y_ref)
        pull_back(nbasis - 2, x_ref)
        pull_back(nbasis - 1, y_ref)
        if f == 0:
            for g in range(filters):
                g_copy(g).wait_recv()
        others = (1 - h) * filters
        cross = [prec[first + f, others + g] for g in range(filters)]
        grad = dot(half[...], cmat[...])
        for g in range(filters):
            grad = grad - cross[g] * recv_g[g].astype(F32)
        e_ref[s, f] = grad.astype(BF16)
        e_copy(f).start()

    def final(f):
        e_copy(f).wait_recv()

        def rows_of(r, n):
            rows = pl.ds(r, n)
            sc = scale[f, rows, :]
            e0 = e_ref[0, f, rows, :].astype(F32)
            e1 = e_ref[1, f, rows, :].astype(F32)
            d0 = sc * noise[0, f, rows, :].astype(F32)
            d1 = sc * noise[1, f, rows, :].astype(F32)
            mu[f, rows, :] = 0.5 * ((e0 + e1) - pri_mu[f, rows, :])
            rho[f, rows, :] = 0.5 * ((e0 * d0 + e1 * d1) - pri_rho[f, rows, :]) + 1.0

        over_rows(rows_of)

    def relay(f):
        rd_copy(f).wait_recv()
        relay_copy(f).start()

    def start_forward(f, between):
        loads[f][1].wait()
        loads[f][2].wait()
        forward(f, between)
        p_copy(f).start()
        d_copy(f).start()

    def nothing():
        pass

    def between_last():
        merge(1)
        twin_sample(0)

    start_forward(0, nothing)
    start_forward(1, lambda: merge(0))
    start_forward(2, between_last)
    for copy in late:
        copy.wait()
    residual(0)
    twin_sample(1)
    merge(2)
    lax.fori_loop(0, filters * K, basis_table, 0)
    basis_move.start()
    residual(1)
    twin_sample(2)
    build(rmat_t, 0, 2, False)
    build(cmat, 2 * nbasis + 1, 2, True)
    residual(2)
    own_prior()
    basis_move.wait()
    relay(0)
    backward(0, lambda: relay(1))
    backward(1, lambda: relay(2))
    backward(2, nothing)
    final(0)
    final(1)
    final(2)

    for f in range(filters):
        for copy in (noise_copy, p_copy, d_copy, q_copy, g_copy, ru_copy, rd_copy, rp_copy, relay_copy, e_copy):
            copy(f).wait_send()


def body(tiles, sky_mean, sky_log_scale, noise_draw, observed, inv_var, intersections, counts, kernels, psf_coeffs, prior_prec):
    filters, side = sky_mean.shape[1], sky_mean.shape[2]
    nbasis, _, taps = kernels.shape
    every, fields = intersections.shape[1], intersections.shape[3]
    exposures = psf_coeffs.shape[0]
    img = (side, side)
    padded = (2, 2 * side, 128)
    vmem = pltpu.VMEM
    smem = pltpu.SMEM
    dma = pltpu.SemaphoreType.DMA
    mu, rho = pl.pallas_call(
        functools.partial(kernel, tiles),
        out_shape=[jax.ShapeDtypeStruct((filters,) + img, F32)] * 2,
        in_specs=[pl.BlockSpec(memory_space=pltpu.HBM)] * 10,
        out_specs=[pl.BlockSpec(memory_space=pltpu.VMEM)] * 2,
        scratch_shapes=[
            vmem((nbasis, 2, taps), F32),
            vmem((4 * nbasis, 128), F32),
            smem((filters, fields, K, intersections.shape[0]), jnp.int32),
            smem((every, counts.shape[0]), jnp.int32),
            vmem((filters, NB, 3, exposures), BF16),
            vmem((filters, NB, 3, exposures), F32),
            smem((filters, NB, 3, exposures), F32),
            smem((every, every), F32),
            vmem((filters * K * 3, 128), F32),
            smem((filters * K * 3, 128), F32),
            vmem((filters,) + img, F32),
            vmem((filters,) + img, F32),
            vmem((2, filters) + img, BF16),
            vmem((filters,) + img, BF16),
            vmem((filters,) + img, BF16),
            vmem((STRIP, 128), F32),
            vmem((nbasis * side, side), BF16),
            vmem((nbasis,) + img, BF16),
            vmem((nbasis * side, side), BF16),
            vmem((nbasis,) + img, BF16),
            vmem(img, BF16),
            vmem(img, BF16),
            vmem((nbasis * side, side), BF16),
            vmem((nbasis, 2, side, 128), F32),
            vmem((K,) + padded, F32),
            vmem((K + 1,) + img, BF16),
            vmem((filters,) + img, BF16),
            vmem((filters, 2) + img, BF16),
            vmem((filters, 2) + img, BF16),
            vmem((filters,) + img, BF16),
            vmem((filters,) + img, BF16),
            vmem((filters,) + img, BF16),
            vmem((filters,) + img, BF16),
            vmem((WINDOW,) + img, BF16),
            vmem((WINDOW,) + img, BF16),
            vmem((WINDOW,) + img, BF16),
            vmem((K, 2, side, 128), F32),
            vmem((side, nbasis * side), BF16),
            vmem((filters,) + img, BF16),
            vmem((filters,) + img, BF16),
            vmem((2, filters) + img, BF16),
            vmem((filters,) + img, F32),
            vmem((filters,) + img, F32),
            dma((4, filters)),
            dma((7,)),
            ]
        + [dma((2, filters))] * 10,
        compiler_params=pltpu.CompilerParams(
            collective_id=0, has_side_effects=True, vmem_limit_bytes=48 * 1024 * 1024
        ),
    )(
        *[
            pltpu.with_memory_space_constraint(value, pltpu.HBM)
            for value in (
                kernels,
                jnp.transpose(intersections, (1, 3, 2, 0)),
                jnp.transpose(counts),
                jnp.transpose(psf_coeffs, (1, 2, 3, 0)),
                prior_prec,
                sky_mean[0],
                sky_log_scale[0],
                noise_draw[0, 0],
                observed[0],
                inv_var[0],
            )
        ]
    )
    return mu[None], rho[None]


def solution(mesh):
    placed = (
        P("tile", "filt", None, None),
        P("tile", "filt", None, None),
        P("mc", "tile", "filt", None, None),
        P("tile", "filt", None, None),
        P("tile", "filt", None, None),
        P(),
        P(),
        P(),
        P(),
        P(),
    )
    return jax.shard_map(
        functools.partial(body, mesh.shape["tile"]),
        mesh=mesh,
        in_specs=placed,
        out_specs=(P("tile", "filt", None, None), P("tile", "filt", None, None)),
        check_vma=False,
    )
```

```python
import functools

import jax
import jax.numpy as jnp
from jax import lax
from jax.experimental import pallas as pl
from jax.experimental.pallas import tpu as pltpu
from jax.sharding import PartitionSpec as P

NB = 6
K = 3
STRIP = 16
REACH = 2
WINDOW = 2 * REACH + 1
MESH = pl.DeviceIdType.MESH
F32 = jnp.float32
BF16 = jnp.bfloat16


def dot(a, b):
    return jnp.dot(a, b, preferred_element_type=F32)


def band_rows(pat, a, side):
    half = side // 2
    start = (16 * a - 12) % half
    rolled = pltpu.roll(pat, start, 1) if start else pat
    lane = lax.broadcasted_iota(jnp.int32, rolled.shape, 1)
    zero = jnp.zeros_like(rolled)
    low = jnp.where(lane < half // 2, rolled, zero)
    high = jnp.where(lane >= half // 2, rolled, zero)
    blocks = half // 16
    if a == 0:
        return low, zero
    if a < blocks - 1:
        return rolled, zero
    if a <= blocks:
        return high, low
    if a < 2 * blocks - 1:
        return zero, rolled
    return zero, high


def kernel(
    tiles,
    kern_hbm,
    inter_hbm,
    count_hbm,
    psf_hbm,
    prec_hbm,
    mean_hbm,
    lsc_hbm,
    noise_hbm,
    obs_hbm,
    ivar_hbm,
    mu,
    rho,
    kern,
    taps,
    inter,
    count,
    psf_b,
    psf_f,
    psf,
    prec,
    basis_v,
    per_basis,
    mean,
    scale,
    noise,
    obs,
    ivar,
    lrow,
    rmat,
    rmat_t,
    cmat,
    cmat_t,
    x_ref,
    y_ref,
    half_blur,
    blur,
    turn,
    placed,
    own,
    send_p,
    recv_p,
    send_d,
    recv_d,
    send_q,
    recv_q,
    near0,
    near1,
    near2,
    moved,
    half,
    send_g,
    recv_g,
    e_ref,
    pri_mu,
    pri_rho,
    in_sem,
    tab_sem,
    noise_sem,
    p_sem,
    d_sem,
    q_sem,
    rp_sem,
    ru_sem,
    rd_sem,
    relay_sem,
    g_sem,
    e_sem,
):
    filters, side = mean.shape[0], mean.shape[1]
    nbasis = rmat_t.shape[0]
    exposures = psf.shape[3]
    near = (near0, near1, near2)
    pad = side // 2
    t = lax.axis_index("tile")
    s = lax.axis_index("mc")
    h = lax.axis_index("filt")
    first = h * filters
    sigma = 1 - 2 * lax.rem(t, 2)
    partner = {"tile": t + sigma}
    ahead = {"tile": lax.rem(t + 2 * sigma + tiles, tiles)}
    behind = {"tile": lax.rem(t - 2 * sigma + tiles, tiles)}
    has_ahead = (t + 2 * sigma >= 0) & (t + 2 * sigma < tiles)
    has_behind = (t - 2 * sigma >= 0) & (t - 2 * sigma < tiles)
    twin = {"mc": 1 - s}
    across = {"filt": 1 - h, "mc": 1 - s}

    def remote(src, dst, sem, f, to):
        return pltpu.make_async_remote_copy(
            src_ref=src,
            dst_ref=dst,
            send_sem=sem.at[0, f],
            recv_sem=sem.at[1, f],
            device_id=to,
            device_id_type=MESH,
        )

    ours = pl.ds(first, filters)
    kern_in = pltpu.make_async_copy(kern_hbm, kern, tab_sem.at[0])
    psf_in = pltpu.make_async_copy(psf_hbm.at[ours], psf_b, tab_sem.at[1])
    inter_in = pltpu.make_async_copy(inter_hbm.at[ours], inter, tab_sem.at[2])
    count_in = pltpu.make_async_copy(count_hbm, count, tab_sem.at[3])
    prec_in = pltpu.make_async_copy(prec_hbm, prec, tab_sem.at[4])
    basis_move = pltpu.make_async_copy(basis_v, per_basis, tab_sem.at[6])
    psf_move = pltpu.make_async_copy(psf_f, psf, tab_sem.at[5])
    for copy in (kern_in, psf_in, inter_in, count_in, prec_in):
        copy.start()
    loads = []
    for f in range(filters):
        loads.append(
            [
                pltpu.make_async_copy(noise_hbm.at[f], noise.at[s, f], in_sem.at[0, f]),
                pltpu.make_async_copy(mean_hbm.at[f], mean.at[f], in_sem.at[1, f]),
                pltpu.make_async_copy(lsc_hbm.at[f], scale.at[f], in_sem.at[2, f]),
            ]
        )
    late = [
        pltpu.make_async_copy(obs_hbm, obs, in_sem.at[3, 0]),
        pltpu.make_async_copy(ivar_hbm, ivar, in_sem.at[3, 1]),
    ]
    for group in loads:
        for copy in group:
            copy.start()
    for copy in late:
        copy.start()

    barrier = pltpu.get_barrier_semaphore()

    def greet(to):
        pl.semaphore_signal(barrier, inc=1, device_id=to, device_id_type=MESH)

    for to in (partner, twin, across):
        greet(to)
    pl.when(has_ahead)(lambda: greet(ahead))
    pl.when(has_behind)(lambda: greet(behind))

    centre_i = lax.broadcasted_iota(jnp.int32, (STRIP, 128), 0)
    lrow[...] = (2 * centre_i + 1 - side).astype(F32) * (1.0 / side)
    centre_j = lax.broadcasted_iota(jnp.int32, (1, side), 1)
    lcol = (2 * centre_j + 1 - side).astype(F32) * (1.0 / side)
    lanes = lax.broadcasted_iota(jnp.int32, (1, 128), 1)
    placed[K] = jnp.zeros((side, side), BF16)
    edge = jnp.zeros((pad, 128), F32)

    def clear_edges(ref, at):
        for lo in range(2):
            ref[at, lo, 0:pad, :] = edge
            ref[at, lo, pad + side : side + 2 * pad, :] = edge

    for q in range(K):
        clear_edges(turn, q)

    def noise_copy(f):
        return remote(noise.at[s, f], noise.at[s, f], noise_sem, f, twin)

    for f in range(filters):
        loads[f][0].wait()
    inner = has_ahead & has_behind
    pl.when(inner)(lambda: pl.semaphore_wait(barrier, 5))
    pl.when(jnp.logical_not(inner))(lambda: pl.semaphore_wait(barrier, 4))
    for f in range(filters):
        noise_copy(f).start()

    blank = jnp.zeros((side, side), BF16)

    @pl.when(jnp.logical_not(has_ahead))
    def _():
        for f in range(filters):
            recv_d[f] = blank
            near[f][REACH + 2 * sigma] = blank

    @pl.when(jnp.logical_not(has_behind))
    def _():
        for f in range(filters):
            recv_q[f] = blank
            near[f][REACH - 2 * sigma] = blank
            near[f][REACH - sigma] = blank

    kern_in.wait()
    taps[...] = jnp.zeros_like(taps)
    ntaps = kern.shape[2]
    for k in range(nbasis):
        taps[2 * k : 2 * k + 2, 0:ntaps] = kern[k]
    swap_i = lax.broadcasted_iota(jnp.int32, (128, 128), 0)
    swap_j = lax.broadcasted_iota(jnp.int32, (128, 128), 1)
    swap = jnp.where(swap_i + swap_j == ntaps - 1, 1.0, 0.0).astype(BF16)
    taps[2 * nbasis : 4 * nbasis, :] = dot(taps[0 : 2 * nbasis, :].astype(BF16), swap)

    def build(dst, from_row, stride, flat):
        def one(k, carry):
            row = taps[from_row + stride * k : from_row + stride * k + 1, :]
            pat = jnp.broadcast_to(row, (16, 128))
            pat = pltpu.roll(pat, 0, 1, stride=1, stride_axis=0)
            for a in range(side // 16):
                left, right = band_rows(pat, a, side)
                for part, lo in ((left, 0), (right, 128)):
                    if flat:
                        at = slice(k * side + 16 * a, k * side + 16 * a + 16)
                        dst[at, lo : lo + 128] = part.astype(BF16)
                    else:
                        dst[k, 16 * a : 16 * a + 16, lo : lo + 128] = part.astype(BF16)
            return carry

        for k in range(nbasis):
            one(k, 0)

    build(rmat, 2 * nbasis, 2, True)
    build(cmat_t, 1, 2, False)

    def over_rows(body, chunk=32):
        for r in range(0, side, chunk):
            body(r, chunk)

    def slot_live(f, q):
        return q < count[first + f, t]

    def slot_exposure(f, q):
        return jnp.clip(inter[f, 0, q, t], 0, exposures - 1)

    def slot_coef(f, q):
        live = slot_live(f, q)
        e = slot_exposure(f, q)
        return [[jnp.where(live, psf[f, b, m, e], 0.0) for m in range(3)] for b in range(NB)]

    def lane_shift(by):
        whole = jnp.right_shift(by, 7)
        rest = jnp.bitwise_and(by, 127)
        right = lanes >= rest
        same = ((whole == 0) & right) | ((whole == -1) & ~right)
        from_high = (whole == -1) & right
        from_low = ((whole == 0) & ~right) | (whole == 1)

        def apply(low, high):
            low = pltpu.roll(low, rest, 1)
            high = pltpu.roll(high, rest, 1)
            none = jnp.zeros_like(low)
            return (
                jnp.where(same, low, jnp.where(from_high, high, none)),
                jnp.where(same, high, jnp.where(from_low, low, none)),
            )

        return apply

    def first_weight(constant, coef, lo):
        return (constant + coef[1] * lrow[...]) + coef[2] * lcol[:, 128 * lo : 128 * lo + 128]

    def forward(f, between):
        def sample_rows(r, n):
            rows = pl.ds(r, n)
            sc = jnp.exp(scale[f, rows, :])
            scale[f, rows, :] = sc
            x_ref[rows, :] = (mean[f, rows, :] + sc * noise[s, f, rows, :].astype(F32)).astype(BF16)

        over_rows(sample_rows)

        if f == 0:
            psf_in.wait()
            psf_f[...] = psf_b[...].astype(F32)
            psf_move.start()
        half_blur[...] = dot(rmat[...], x_ref[...]).astype(BF16)
        for k in range(nbasis):
            image = dot(half_blur[k * side : (k + 1) * side, :], cmat_t[k])
            blur[k, 0] = image[:, 0:128]
            blur[k, 1] = image[:, 128:256]

        between()

        def slot(q, carry):
            coef = slot_coef(f, q)
            oy = inter[f, 1, q, t]
            ox = inter[f, 2, q, t]
            kb = [inter[f, 3 + b, q, t] for b in range(NB)]
            up = oy.astype(F32) * (2.0 / side)
            over = ox.astype(F32) * (2.0 / side)
            c0 = [coef[b][0] + coef[b][1] * up + coef[b][2] * over for b in range(NB)]
            weight = [[first_weight(c0[b], coef[b], lo) for lo in range(2)] for b in range(NB)]
            step = [coef[b][1] * (2.0 * STRIP / side) for b in range(NB)]
            move = lane_shift(ox)

            def mix_rows(i, weight):
                r = i * STRIP
                for lo in range(2):
                    acc = None
                    for b in range(NB):
                        term = weight[b][lo] * blur[kb[b], lo, pl.ds(r, STRIP), :]
                        acc = term if acc is None else acc + term
                    turn[q, lo, pl.ds(pad + r, STRIP), :] = acc
                return [[weight[b][lo] + step[b] for lo in range(2)] for b in range(NB)]

            for i in range(side // STRIP):
                weight = mix_rows(i, weight)

            def place_rows(r, n):
                low, high = move(*[turn[q, lo, pl.ds(pad - oy + r, n), :] for lo in range(2)])
                placed[q, pl.ds(r, n), 0:128] = low.astype(BF16)
                placed[q, pl.ds(r, n), 128:256] = high.astype(BF16)

            for r in range(0, side, 64):
                place_rows(r, 64)
            return carry

        for q in range(K):
            slot(q, 0)
        place = [jnp.where(slot_live(f, q), inter[f, 0, q, t] - t, WINDOW) for q in range(K)]

        def pick(d):
            at = K
            for q in range(K):
                at = jnp.where(place[q] == d, q, at)
            return placed[at]

        own[f] = pick(0)
        send_p[f, 0] = pick(sigma)
        send_p[f, 1] = pick(-sigma)
        send_d[f] = pick(-2 * sigma)
        send_q[f] = pick(2 * sigma)

    def p_copy(f):
        return remote(send_p.at[f], recv_p.at[f], p_sem, f, partner)

    def d_copy(f):
        return remote(send_d.at[f], recv_d.at[f], d_sem, f, behind)

    def q_copy(f):
        return remote(send_q.at[f], recv_q.at[f], q_sem, f, ahead)

    def merge(f):
        p_copy(f).wait_recv()

        def rows_of(r, n):
            rows = pl.ds(r, n)
            joined = send_q[f, rows, :].astype(F32) + recv_p[f, 1, rows, :].astype(F32)
            send_q[f, rows, :] = joined.astype(BF16)

        over_rows(rows_of)
        pl.when(has_ahead)(lambda: q_copy(f).start())

    def g_copy(f):
        return remote(send_g.at[f], recv_g.at[f], g_sem, f, across)

    def twin_sample(f):
        noise_copy(f).wait_recv()

        def twin_rows(r, n):
            rows = pl.ds(r, n)
            other = noise[1 - s, f, rows, :].astype(F32)
            send_g[f, rows, :] = (mean[f, rows, :] + scale[f, rows, :] * other).astype(BF16)

        over_rows(twin_rows)
        g_copy(f).start()

    def rp_copy(f):
        return remote(near[f].at[REACH], near[f].at[REACH - sigma], rp_sem, f, partner)

    def ru_copy(f):
        return remote(near[f].at[REACH], near[f].at[REACH - 2 * sigma], ru_sem, f, ahead)

    def rd_copy(f):
        return remote(near[f].at[REACH], near[f].at[REACH + 2 * sigma], rd_sem, f, behind)

    def relay_copy(f):
        return remote(near[f].at[REACH + 2 * sigma], near[f].at[REACH + sigma], relay_sem, f, partner)

    def residual(f):
        pl.when(has_ahead)(lambda: d_copy(f).wait_recv())
        pl.when(has_behind)(lambda: q_copy(f).wait_recv())

        def rows_of(r, n):
            rows = pl.ds(r, n)
            pred = own[f, rows, :].astype(F32) + recv_p[f, 0, rows, :].astype(F32)
            pred = pred + recv_d[f, rows, :].astype(F32) + recv_q[f, rows, :].astype(F32)
            res = ivar[f, rows, :].astype(F32) * (obs[f, rows, :].astype(F32) - pred)
            near[f][REACH, rows, :] = res.astype(BF16)

        over_rows(rows_of)
        pl.when(has_ahead)(lambda: ru_copy(f).start())
        pl.when(has_behind)(lambda: rd_copy(f).start())
        rp_copy(f).start()

    def basis_table(fq, carry):
        f = fq // K
        q = fq - K * f
        coef = slot_coef(f, q)
        up = inter[f, 1, q, t].astype(F32) * (2.0 / side)
        across_by = inter[f, 2, q, t].astype(F32) * (2.0 / side)
        kb = [inter[f, 3 + b, q, t] for b in range(NB)]
        for b in range(NB):
            coef[b][0] = coef[b][0] + coef[b][1] * up + coef[b][2] * across_by
        for m in range(3):
            total = jnp.zeros((1, 128), F32)
            for b in range(NB):
                total = total + jnp.where(lanes == kb[b], coef[b][m], 0.0)
            basis_v[pl.ds(3 * fq + m, 1), :] = total
        return carry

    def own_prior():
        rows_in = [[prec[first + f, first + g] for g in range(filters)] for f in range(filters)]

        def rows_of(r, n):
            rows = pl.ds(r, n)
            sam = [[None] * filters for _ in range(2)]
            dev = [[None] * filters for _ in range(2)]
            for g in range(filters):
                mn, sc = mean[g, rows, :], scale[g, rows, :]
                for which in range(2):
                    dev[which][g] = sc * noise[which, g, rows, :].astype(F32)
                    sam[which][g] = mn + dev[which][g]
            for f in range(filters):
                pri = []
                for which in range(2):
                    total = None
                    for g in range(filters):
                        term = rows_in[f][g] * sam[which][g]
                        total = term if total is None else total + term
                    pri.append(total)
                pri_mu[f, rows, :] = pri[0] + pri[1]
                pri_rho[f, rows, :] = pri[0] * dev[0][f] + pri[1] * dev[1][f]

        over_rows(rows_of, 16)

    def e_copy(f):
        return remote(e_ref.at[s, f], e_ref.at[s, f], e_sem, f, twin)

    def backward(f, between):
        rp_copy(f).wait_recv()

        @pl.when(has_behind)
        def _():
            ru_copy(f).wait_recv()
            relay_copy(f).wait_recv()


        def pull(q, carry):
            at = jnp.clip(inter[f, 0, q, t] - t + REACH, 0, WINDOW - 1)
            move = lane_shift(-inter[f, 2, q, t])

            def pull_rows(r, n):
                image = near[f][at, pl.ds(r, n), :].astype(F32)
                low, high = move(image[:, 0:128], image[:, 128:256])
                turn[q, 0, pl.ds(pad + r, n), :] = low
                turn[q, 1, pl.ds(pad + r, n), :] = high

            over_rows(pull_rows, 64)
            oy = inter[f, 1, q, t]

            def settle_rows(r, n):
                for lo in range(2):
                    moved[q, lo, pl.ds(r, n), :] = turn[q, lo, pl.ds(pad + oy + r, n), :]

            over_rows(settle_rows, 64)
            return carry

        for q in range(K):
            pull(q, 0)

        def weigh(k, dst):
            coef = [[per_basis[(f * K + q) * 3 + m, k] for m in range(3)] for q in range(K)]
            weight = [[first_weight(coef[q][0], coef[q], lo) for lo in range(2)] for q in range(K)]
            step = [coef[q][1] * (2.0 * STRIP / side) for q in range(K)]
            for r in range(0, side, STRIP):
                for lo in range(2):
                    acc = None
                    for q in range(K):
                        term = weight[q][lo] * moved[q, lo, r : r + STRIP, :]
                        acc = term if acc is None else acc + term
                        if r + STRIP < side:
                            weight[q][lo] = weight[q][lo] + step[q]
                    dst[r : r + STRIP, 128 * lo : 128 * lo + 128] = acc.astype(BF16)

        def pull_back(k, src):
            half[:, k * side : (k + 1) * side] = dot(rmat_t[k], src[...]).astype(BF16)

        weigh(0, x_ref)

        def pair(j, carry):
            weigh(2 * j + 1, y_ref)
            pull_back(2 * j, x_ref)
            weigh(2 * j + 2, x_ref)
            pull_back(2 * j + 1, y_ref)
            return carry

        for j in range(nbasis // 2 - 1):
            pair(j, 0)
        between()
        weigh(nbasis - 1, y_ref)
        pull_back(nbasis - 2, x_ref)
        pull_back(nbasis - 1, y_ref)
        if f == 0:
            for g in range(filters):
                g_copy(g).wait_recv()
        others = (1 - h) * filters
        cross = [prec[first + f, others + g] for g in range(filters)]
        grad = dot(half[...], cmat[...])
        for g in range(filters):
            grad = grad - cross[g] * recv_g[g].astype(F32)
        e_ref[s, f] = grad.astype(BF16)
        e_copy(f).start()

    def final(f):
        e_copy(f).wait_recv()

        def rows_of(r, n):
            rows = pl.ds(r, n)
            sc = scale[f, rows, :]
            e0 = e_ref[0, f, rows, :].astype(F32)
            e1 = e_ref[1, f, rows, :].astype(F32)
            d0 = sc * noise[0, f, rows, :].astype(F32)
            d1 = sc * noise[1, f, rows, :].astype(F32)
            mu[f, rows, :] = 0.5 * ((e0 + e1) - pri_mu[f, rows, :])
            rho[f, rows, :] = 0.5 * ((e0 * d0 + e1 * d1) - pri_rho[f, rows, :]) + 1.0

        over_rows(rows_of)

    def relay(f):
        @pl.when(has_ahead)
        def _():
            rd_copy(f).wait_recv()
            relay_copy(f).start()

    def start_forward(f, between):
        loads[f][1].wait()
        loads[f][2].wait()
        forward(f, between)
        p_copy(f).start()
        pl.when(has_behind)(lambda: d_copy(f).start())

    def nothing():
        pass

    def between_first():
        inter_in.wait()
        count_in.wait()
        prec_in.wait()
        psf_move.wait()

    def between_last():
        merge(1)
        twin_sample(0)

    start_forward(0, between_first)
    start_forward(1, lambda: merge(0))
    start_forward(2, between_last)
    for copy in late:
        copy.wait()
    residual(0)
    twin_sample(1)
    merge(2)
    lax.fori_loop(0, filters * K, basis_table, 0)
    basis_move.start()
    residual(1)
    twin_sample(2)
    build(rmat_t, 0, 2, False)
    build(cmat, 2 * nbasis + 1, 2, True)
    residual(2)
    own_prior()
    basis_move.wait()
    relay(0)
    backward(0, lambda: relay(1))
    backward(1, lambda: relay(2))
    backward(2, nothing)
    final(0)
    final(1)
    final(2)

    for f in range(filters):
        for copy in (noise_copy, p_copy, g_copy, rp_copy, e_copy):
            copy(f).wait_send()

    @pl.when(has_ahead)
    def _():
        for f in range(filters):
            for copy in (q_copy, ru_copy, relay_copy):
                copy(f).wait_send()

    @pl.when(has_behind)
    def _():
        for f in range(filters):
            for copy in (d_copy, rd_copy):
                copy(f).wait_send()


def body(tiles, sky_mean, sky_log_scale, noise_draw, observed, inv_var, intersections, counts, kernels, psf_coeffs, prior_prec):
    filters, side = sky_mean.shape[1], sky_mean.shape[2]
    nbasis, _, taps = kernels.shape
    every, fields = intersections.shape[1], intersections.shape[3]
    exposures = psf_coeffs.shape[0]
    img = (side, side)
    padded = (2, 2 * side, 128)
    vmem = pltpu.VMEM
    smem = pltpu.SMEM
    dma = pltpu.SemaphoreType.DMA
    mu, rho = pl.pallas_call(
        functools.partial(kernel, tiles),
        out_shape=[jax.ShapeDtypeStruct((filters,) + img, F32)] * 2,
        in_specs=[pl.BlockSpec(memory_space=pltpu.HBM)] * 10,
        out_specs=[pl.BlockSpec(memory_space=pltpu.VMEM)] * 2,
        scratch_shapes=[
            vmem((nbasis, 2, taps), F32),
            vmem((4 * nbasis, 128), F32),
            smem((filters, fields, K, intersections.shape[0]), jnp.int32),
            smem((every, counts.shape[0]), jnp.int32),
            vmem((filters, NB, 3, exposures), BF16),
            vmem((filters, NB, 3, exposures), F32),
            smem((filters, NB, 3, exposures), F32),
            smem((every, every), F32),
            vmem((filters * K * 3, 128), F32),
            smem((filters * K * 3, 128), F32),
            vmem((filters,) + img, F32),
            vmem((filters,) + img, F32),
            vmem((2, filters) + img, BF16),
            vmem((filters,) + img, BF16),
            vmem((filters,) + img, BF16),
            vmem((STRIP, 128), F32),
            vmem((nbasis * side, side), BF16),
            vmem((nbasis,) + img, BF16),
            vmem((nbasis * side, side), BF16),
            vmem((nbasis,) + img, BF16),
            vmem(img, BF16),
            vmem(img, BF16),
            vmem((nbasis * side, side), BF16),
            vmem((nbasis, 2, side, 128), F32),
            vmem((K,) + padded, F32),
            vmem((K + 1,) + img, BF16),
            vmem((filters,) + img, BF16),
            vmem((filters, 2) + img, BF16),
            vmem((filters, 2) + img, BF16),
            vmem((filters,) + img, BF16),
            vmem((filters,) + img, BF16),
            vmem((filters,) + img, BF16),
            vmem((filters,) + img, BF16),
            vmem((WINDOW,) + img, BF16),
            vmem((WINDOW,) + img, BF16),
            vmem((WINDOW,) + img, BF16),
            vmem((K, 2, side, 128), F32),
            vmem((side, nbasis * side), BF16),
            vmem((filters,) + img, BF16),
            vmem((filters,) + img, BF16),
            vmem((2, filters) + img, BF16),
            vmem((filters,) + img, F32),
            vmem((filters,) + img, F32),
            dma((4, filters)),
            dma((7,)),
            ]
        + [dma((2, filters))] * 10,
        compiler_params=pltpu.CompilerParams(
            collective_id=0, has_side_effects=True, vmem_limit_bytes=48 * 1024 * 1024
        ),
    )(
        *[
            pltpu.with_memory_space_constraint(value, pltpu.HBM)
            for value in (
                kernels,
                jnp.transpose(intersections, (1, 3, 2, 0)),
                jnp.transpose(counts),
                jnp.transpose(psf_coeffs, (1, 2, 3, 0)),
                prior_prec,
                sky_mean[0],
                sky_log_scale[0],
                noise_draw[0, 0],
                observed[0],
                inv_var[0],
            )
        ]
    )
    return mu[None], rho[None]


def solution(mesh):
    placed = (
        P("tile", "filt", None, None),
        P("tile", "filt", None, None),
        P("mc", "tile", "filt", None, None),
        P("tile", "filt", None, None),
        P("tile", "filt", None, None),
        P(),
        P(),
        P(),
        P(),
        P(),
    )
    return jax.shard_map(
        functools.partial(body, mesh.shape["tile"]),
        mesh=mesh,
        in_specs=placed,
        out_specs=(P("tile", "filt", None, None), P("tile", "filt", None, None)),
        check_vma=False,
    )
```
